32 devices in a mesh: fsdp: 8 (over z, x), seq: 4 (over y, core).
Axes of the slice: x: 2, y: 2, z: 4, core: 2. Of those that a mesh axis runs over, the one named last changes fastest.
Arguments:
- tokens: bfloat16 [16, 1024, 1024], P('fsdp', 'seq'), may hold values from -6 to 6
- w_query: bfloat16 [1024, 1024], P('fsdp'), may hold values from -0.1875 to 0.1875
- w_key: bfloat16 [1024, 512], P('fsdp'), may hold values from -0.1875 to 0.1875
- w_value: bfloat16 [1024, 512], P('fsdp'), may hold values from -0.1875 to 0.1875
- w_out: bfloat16 [1024, 1024], P('fsdp'), may hold values from -0.75 to 0.75
- w_gate: bfloat16 [1024, 4608], P('fsdp'), may hold values from -0.1875 to 0.1875
- w_up: bfloat16 [1024, 4608], P('fsdp'), may hold values from -0.1875 to 0.1875
- w_down: bfloat16 [4608, 1024], P('fsdp'), may hold values from -0.125 to 0.125
- attn_gain: bfloat16 [1024], P('fsdp'), may hold values from 0.099609375 to 1.8984375
- ffn_gain: bfloat16 [1024], P('fsdp'), may hold values from 0.099609375 to 1.8984375
- qk_gain: bfloat16 [2, 64], replicated, may hold values from 0.099609375 to 1.8984375
- cotangent: bfloat16 [16, 1024, 1024], P('fsdp', 'seq'), may hold values from -6 to 6
Outputs:
- out: bfloat16 [16, 1024, 1024], P('fsdp', 'seq')
- grad_tokens: float32 [16, 1024, 1024], P('fsdp', 'seq')
- grad_query: float32 [1024, 1024], P('fsdp')
- grad_key: float32 [1024, 512], P('fsdp')
- grad_value: float32 [1024, 512], P('fsdp')
- grad_out: float32 [1024, 1024], P('fsdp')
- grad_gate: float32 [1024, 4608], P('fsdp')
- grad_up: float32 [1024, 4608], P('fsdp')
- grad_down: float32 [4608, 1024], P('fsdp')
- grad_attn_gain: float32 [1024], P('fsdp')
- grad_ffn_gain: float32 [1024], P('fsdp')
- grad_qk_gain: float32 [2, 64], replicated
The draws below stay inside these ranges and needn't reach their ends.
All inputs are finite; a program needn't handle non-finite values.
Results may differ from the reference program's by a relative error of at most 0.022.
Values may be sent and summed in bfloat16 or wider, within the bound.
No kernel may reach another device: no remote copies, remote signals or barrier semaphores. Data moves between devices by JAX's collectives and lax.ppermute only.
A program may use at most 192 MiB of HBM per device.

```python
import jax
import jax.numpy as jnp
from jax import lax

D = 1024
H = 16
KV = 8
HD = 64
FF = 4608
LEN = 1024
SEQS = 16


def shard_levels(key, dims, split, smallest, high):
    level, own = 1.0, jax.random.fold_in(key, 6)
    for axis_at, parts in split:
        heights = jnp.exp(jax.random.uniform(jax.random.fold_in(own, axis_at), (parts,), jnp.float32, smallest / len(split), high / len(split)))
        level = level * jnp.repeat(heights, dims[axis_at] // parts).reshape([-1 if axis == axis_at else 1 for axis in range(len(dims))])
    return level


def centred(own_key, extent, width, limit, split=(), kind=jnp.bfloat16):
    entries = jax.random.normal(own_key, extent, jnp.float32) * width
    if len(split) > 0:
        entries = shard_levels(own_key, extent, split, -0.22, 0.18) * entries
    return jnp.clip(entries, min=-limit, max=limit).astype(kind)


def setup_inputs(seed: int = 0) -> dict:
    key_list = jax.random.split(jax.random.key(seed), 13)
    tokens = centred(key_list[0], (SEQS, LEN, D), 1.0, 6.0, ((0, 8), (1, 4)))
    w_query = centred(key_list[1], (D, H * HD), D ** -0.5, 0.1875, ((0, 8),))
    w_key = centred(key_list[2], (D, KV * HD), D ** -0.5, 0.1875, ((0, 8),))
    w_value = centred(key_list[3], (D, KV * HD), D ** -0.5, 0.1875, ((0, 8),))
    w_out = centred(key_list[4], (H * HD, D), (H * HD // 16) ** -0.5, 0.75, ((0, 8),))
    w_gate = centred(key_list[5], (D, FF), D ** -0.5, 0.1875, ((0, 8),))
    w_up = centred(key_list[6], (D, FF), D ** -0.5, 0.1875, ((0, 8),))
    w_down = centred(key_list[7], (FF, D), (FF // 2) ** -0.5, 0.125, ((0, 8),))
    attn_gain = jnp.clip(1.0 + 0.18 * jax.random.normal(key_list[8], (D,), jnp.float32), 0.099609375, 1.8984375).astype(jnp.bfloat16)
    ffn_gain = jnp.clip(1.0 + 0.18 * jax.random.normal(key_list[9], (D,), jnp.float32), 0.099609375, 1.8984375).astype(jnp.bfloat16)
    qk_gain = jnp.clip(1.0 + 0.18 * jax.random.normal(key_list[10], (2, HD), jnp.float32), 0.099609375, 1.8984375).astype(jnp.bfloat16)
    cotangent = centred(key_list[11], (SEQS, LEN, D), 1.0, 6.0, ((0, 8), (1, 4)))
    return dict(tokens=tokens, w_query=w_query, w_key=w_key, w_value=w_value, w_out=w_out, w_gate=w_gate, w_up=w_up, w_down=w_down, attn_gain=attn_gain, ffn_gain=ffn_gain, qk_gain=qk_gain, cotangent=cotangent)


RMS_EPSILON = 1e-05
ROPE_THETA = 1000000.0
HIGHEST = lax.Precision.HIGHEST

@jax.custom_vjp
def low(v):
    return lax.optimization_barrier(v.astype(jnp.bfloat16)).astype(jnp.float32)

@jax.custom_vjp
def low_back(v):
    return v

def low_keep(v):
    return (low(v), None)

def low_pass(kept, grad):
    return (grad,)

def back_keep(v):
    return (v, None)

def back_low(kept, grad):
    return (low(grad),)
low.defvjp(low_keep, low_pass)
low_back.defvjp(back_keep, back_low)

def rms_scale(values):
    return lax.rsqrt(lax.optimization_barrier(jnp.mean(values * values, axis=-1, keepdims=True)) + RMS_EPSILON)

def rope_tables(positions, head_size):
    half_size = head_size // 2
    freqs = ROPE_THETA ** (-(jnp.arange(half_size, dtype=jnp.float32) * 2.0) / head_size)
    angles = positions.astype(jnp.float32)[:, None] * freqs[None, :]
    angles = jnp.concatenate([angles, angles], axis=-1)
    return (jnp.cos(angles), jnp.sin(angles))

def rotate(values):
    half_size = values.shape[-1] // 2
    return jnp.concatenate([-values[..., half_size:], values[..., :half_size]], axis=-1)

def matmul_high(left_side, right_side):
    return jnp.dot(left_side, right_side, precision=HIGHEST)

def head_rope(flat, gain, cosine, sine):
    shaped = flat.reshape(flat.shape[0], -1, HD)
    normed = shaped * rms_scale(shaped) * gain
    turned = normed * cosine[:, None, :] + rotate(normed) * sine[:, None, :]
    return turned.reshape(flat.shape)

def block(params, inputs):
    w_query, w_key, w_value, w_out, w_gate, w_up, w_down, attn_gain, ffn_gain, qk_gain = params
    length = inputs.shape[0]
    normed = low(inputs * rms_scale(inputs) * attn_gain)
    query_raw = low_back(matmul_high(normed, w_query))
    key_raw = low_back(matmul_high(normed, w_key))
    value_raw = matmul_high(normed, w_value)
    cosine, sine = rope_tables(jnp.arange(length), HD)
    queries = low_back(low(head_rope(query_raw, qk_gain[0], cosine, sine)))
    keys = low_back(low(head_rope(key_raw, qk_gain[1], cosine, sine)))
    values = low_back(low(value_raw))
    group = H // KV
    query_heads = queries.reshape(length, KV, group, HD)
    key_heads = keys.reshape(length, KV, HD)
    value_heads = values.reshape(length, KV, HD)
    scores = jnp.einsum('qkgd,skd->kgqs', query_heads, key_heads, precision=HIGHEST)
    scores = low_back(scores * HD ** (-0.5))
    positions = jnp.arange(length)
    causal = positions[:, None] >= positions[None, :]
    probs = low(jax.nn.softmax(jnp.where(causal, scores, -1e+30), axis=-1))
    mixed = jnp.einsum('kgqs,skd->qkgd', probs, value_heads, precision=HIGHEST)
    mixed = low_back(low(mixed.reshape(length, H * HD)))
    branch = low_back(matmul_high(mixed, w_out))
    middle = inputs + branch
    normed_two = low(middle * rms_scale(middle) * ffn_gain)
    gate = low_back(matmul_high(normed_two, w_gate))
    upward = low_back(matmul_high(normed_two, w_up))
    hidden = low(jax.nn.silu(gate) * upward)
    return middle + matmul_high(hidden, w_down)

def reference(tokens, w_query, w_key, w_value, w_out, w_gate, w_up, w_down, attn_gain, ffn_gain, qk_gain, cotangent):
    params = (w_query.astype(jnp.float32), w_key.astype(jnp.float32), w_value.astype(jnp.float32), w_out.astype(jnp.float32), w_gate.astype(jnp.float32), w_up.astype(jnp.float32), w_down.astype(jnp.float32), attn_gain.astype(jnp.float32), ffn_gain.astype(jnp.float32), qk_gain.astype(jnp.float32))

    def one_sequence(running, pieces):
        seq_tokens, seq_cotangent = pieces
        result, pullback = jax.vjp(block, params, seq_tokens.astype(jnp.float32))
        grad_params, grad_inputs = pullback(seq_cotangent.astype(jnp.float32))
        running = jax.tree.map(lambda before, extra_part: before + extra_part, running, grad_params)
        return (running, (result.astype(jnp.bfloat16), grad_inputs))
    zeros = jax.tree.map(jnp.zeros_like, params)
    totals, (outputs, grad_inputs) = lax.scan(one_sequence, zeros, (tokens, cotangent))
    return (outputs, grad_inputs, totals[0], totals[1], totals[2], totals[3], totals[4], totals[5], totals[6], totals[7], totals[8], totals[9])
```

```python
import functools

import jax
import jax.numpy as jnp
from jax import lax
from jax.sharding import PartitionSpec as P

HD = 64


RMS_EPSILON = 1e-05
ROPE_THETA = 1000000.0
NEG_LARGE = -1e30


def rms_scale(values):
    return lax.rsqrt(jnp.mean(values * values, axis=-1, keepdims=True) + RMS_EPSILON)


def rope_tables(positions, head_size):
    half_size = head_size // 2
    freqs = ROPE_THETA ** (-(jnp.arange(half_size, dtype=jnp.float32) * 2.0) / head_size)
    angles = positions.astype(jnp.float32)[:, None] * freqs[None, :]
    angles = jnp.concatenate([angles, angles], axis=-1)
    return (jnp.cos(angles), jnp.sin(angles))


def rotate(values):
    half_size = values.shape[-1] // 2
    return jnp.concatenate([-values[..., half_size:], values[..., :half_size]], axis=-1)


def rotate_back(values):
    half_size = values.shape[-1] // 2
    return jnp.concatenate([values[..., half_size:], -values[..., :half_size]], axis=-1)


def head_rope(flat, gain, cosine, sine):
    shaped = flat.reshape(flat.shape[:-1] + (-1, HD))
    scale = rms_scale(shaped)
    normed = shaped * scale * gain
    turned = normed * cosine[:, None, :] + rotate(normed) * sine[:, None, :]
    return (turned.reshape(flat.shape), scale)


def head_rope_back(grad_flat, flat, scale, gain, cosine, sine):
    shaped = flat.reshape(flat.shape[:-1] + (-1, HD))
    grad_turned = grad_flat.reshape(shaped.shape)
    grad_normed = grad_turned * cosine[:, None, :] + rotate_back(grad_turned * sine[:, None, :])
    grad_gain = jnp.sum(grad_normed * shaped * scale, axis=(0, 1, 2))
    weighted = grad_normed * gain
    grad_shaped = scale * weighted - shaped * scale**3 * jnp.mean(
        weighted * shaped, axis=-1, keepdims=True
    )
    return (grad_shaped.reshape(flat.shape), grad_gain)


def norm_back(grad, values, scale, gain):
    weighted = grad * gain
    grad_values = scale * weighted - values * scale**3 * jnp.mean(
        weighted * values, axis=-1, keepdims=True
    )
    grad_gain = jnp.sum(grad * values * scale, axis=(0, 1))
    return (grad_values, grad_gain)


def to_blocks(flat, count, kv_heads):
    batch, length, width = flat.shape
    group = width // (kv_heads * HD)
    shaped = flat.reshape(batch, count, length // count, kv_heads, group, HD)
    return jnp.moveaxis(shaped, 1, 0)


def split_heads(query_flat, key_flat, value_flat):
    batch, length, width = query_flat.shape
    kv_heads = key_flat.shape[2] // HD
    block_rows = min(512, length)
    count = length // block_rows
    query_blocks = to_blocks(query_flat, count, kv_heads)
    key_heads = key_flat.reshape(batch, length, kv_heads, HD)
    value_heads = value_flat.reshape(batch, length, kv_heads, HD)
    starts = jnp.arange(count) * block_rows
    return (query_blocks, key_heads, value_heads, starts)


def block_scores(query_block, key_heads, start):
    block_rows = query_block.shape[1]
    scores = jnp.einsum(
        "bqkgd,bskd->bkgqs", query_block, key_heads, preferred_element_type=jnp.float32
    ) * HD ** (-0.5)
    rows = start + jnp.arange(block_rows)
    columns = jnp.arange(key_heads.shape[1])
    causal = rows[:, None] >= columns[None, :]
    return (scores, causal)


def attend(parts):
    query_flat, key_flat, value_flat = parts
    batch, length, width = query_flat.shape
    query_blocks, key_heads, value_heads, starts = split_heads(query_flat, key_flat, value_flat)

    def one_block(pieces):
        query_block, start = pieces
        scores, causal = block_scores(query_block, key_heads, start)
        scores = jnp.where(causal, scores, NEG_LARGE)
        row_max = jnp.max(scores, axis=-1, keepdims=True)
        exp_part = jnp.exp(scores - row_max)
        row_sum = jnp.sum(exp_part, axis=-1, keepdims=True)
        probs = (exp_part / row_sum).astype(jnp.bfloat16)
        mixed = jnp.einsum(
            "bkgqs,bskd->bqkgd", probs, value_heads, preferred_element_type=jnp.float32
        )
        return (mixed.astype(jnp.bfloat16), (row_max + jnp.log(row_sum))[..., 0])

    mixed, log_sums = lax.map(one_block, (query_blocks, starts))
    mixed = jnp.moveaxis(mixed, 0, 1).reshape(batch, length, width)
    kv_heads = log_sums.shape[2]
    group = log_sums.shape[3]
    log_sums = jnp.moveaxis(log_sums, 0, 3).reshape(batch, kv_heads, group, length)
    return (mixed, log_sums, query_flat, key_flat, value_flat)


def attend_back(query_flat, key_flat, value_flat, log_sums, grad_mixed):
    batch, length, width = query_flat.shape
    query_blocks, key_heads, value_heads, starts = split_heads(query_flat, key_flat, value_flat)
    count = starts.shape[0]
    kv_heads = key_heads.shape[2]
    grad_blocks = to_blocks(grad_mixed, count, kv_heads)
    sum_blocks = jnp.moveaxis(log_sums.reshape(log_sums.shape[:3] + (count, length // count)), 3, 0)
    head_scale = HD ** (-0.5)

    def one_block(carry, pieces):
        grad_keys, grad_values = carry
        query_block, grad_block, sums_block, start = pieces
        scores, causal = block_scores(query_block, key_heads, start)
        probs = jnp.where(causal, jnp.exp(scores - sums_block[..., None]), 0.0)
        grad_values = grad_values + jnp.einsum(
            "bkgqs,bqkgd->bskd",
            probs.astype(jnp.bfloat16),
            grad_block,
            preferred_element_type=jnp.float32,
        )
        grad_probs = jnp.einsum(
            "bqkgd,bskd->bkgqs", grad_block, value_heads, preferred_element_type=jnp.float32
        )
        inner = jnp.sum(probs * grad_probs, axis=-1, keepdims=True)
        grad_scores = (probs * (grad_probs - inner)).astype(jnp.bfloat16)
        grad_query = (
            jnp.einsum(
                "bkgqs,bskd->bqkgd", grad_scores, key_heads, preferred_element_type=jnp.float32
            )
            * head_scale
        )
        grad_keys = (
            grad_keys
            + jnp.einsum(
                "bkgqs,bqkgd->bskd", grad_scores, query_block, preferred_element_type=jnp.float32
            )
            * head_scale
        )
        return ((grad_keys, grad_values), grad_query.astype(jnp.bfloat16))

    zero_heads = jnp.zeros(key_heads.shape, jnp.float32)
    (grad_keys, grad_values), grad_query = lax.scan(
        one_block, (zero_heads, zero_heads), (query_blocks, grad_blocks, sum_blocks, starts)
    )
    grad_query = jnp.moveaxis(grad_query, 0, 1).reshape(batch, length, width)
    grad_keys = grad_keys.reshape(key_flat.shape).astype(jnp.bfloat16)
    grad_values = grad_values.reshape(value_flat.shape).astype(jnp.bfloat16)
    return (grad_query, grad_keys, grad_values)


def bits_of(count):
    return [1 << i for i in range(count.bit_length() - 1)]


def swap(values, bit, count):
    return lax.ppermute(values, "seq", [(i, i ^ bit) for i in range(count)])


def gather_blocks(block, count):
    blocks = {0: block}
    for bit in reversed(bits_of(count)):
        for at in list(blocks):
            blocks[at | bit] = swap(blocks[at], bit, count)
    return blocks


def scatter_blocks(blocks, count):
    blocks = dict(blocks)
    for bit in bits_of(count):
        kept = {}
        for at in blocks:
            if not at & bit:
                arrived = swap(blocks[at | bit].astype(jnp.bfloat16), bit, count)
                kept[at] = blocks[at].astype(jnp.float32) + arrived.astype(jnp.float32)
        blocks = kept
    return blocks[0]


def in_order(blocks, own, count):
    batch, rows, width = blocks[0].shape
    whole = jnp.zeros((batch, count * rows, width), blocks[0].dtype)
    for at in range(count):
        whole = lax.dynamic_update_slice(whole, blocks[at], (0, (own ^ at) * rows, 0))
    return whole


def from_order(whole, own, count):
    rows = whole.shape[1] // count
    return {
        at: lax.dynamic_slice_in_dim(whole, (own ^ at) * rows, rows, axis=1) for at in range(count)
    }


def dot(left, right):
    return jnp.dot(left, right, preferred_element_type=jnp.float32)


def dot_t(left, right):
    return lax.dot_general(
        left, right, (((1,), (1,)), ((), ())), preferred_element_type=jnp.float32
    )


def t_dot(left, right):
    return lax.dot_general(
        left, right, (((0,), (0,)), ((), ())), preferred_element_type=jnp.float32
    )


def per_device(
    fsdp,
    seq,
    tokens,
    w_query,
    w_key,
    w_value,
    w_out,
    w_gate,
    w_up,
    w_down,
    attn_gain,
    ffn_gain,
    qk_gain,
    cotangent,
):
    bf16 = jnp.bfloat16
    f32 = jnp.float32
    own = lax.axis_index("seq")
    batch, rows, width = tokens.shape
    length = rows * seq
    count = batch * length
    part = w_query.shape[0]
    q_width = w_query.shape[1] // seq
    kv_width = w_key.shape[1] // seq
    o_width = w_out.shape[1] // seq
    units = w_down.shape[0] // seq
    local = units * fsdp

    def columns(weight, size):
        return lax.dynamic_slice_in_dim(weight, own * size, size, axis=1)

    gains = jnp.stack([attn_gain, ffn_gain], axis=1)
    first = jnp.concatenate(
        [
            columns(w_query, q_width),
            columns(w_key, kv_width),
            columns(w_value, kv_width),
            columns(w_out, o_width),
            jnp.pad(gains, ((0, 0), (0, 126))),
        ],
        axis=1,
    )
    first_all = lax.all_gather(first, "fsdp", axis=0, tiled=True)
    qkv_width = q_width + 2 * kv_width
    w_qkv = first_all[:, :qkv_width]
    out_cols = first_all[:, qkv_width : qkv_width + o_width]
    attn_full = first_all[:, qkv_width + o_width].astype(f32)
    ffn_full = first_all[:, qkv_width + o_width + 1].astype(f32)

    def pick(weight):
        split = weight.reshape(part, fsdp, seq, units)
        return lax.dynamic_index_in_dim(split, own, axis=2, keepdims=False).reshape(part, local)

    down_own = lax.dynamic_slice_in_dim(w_down, own * units, units, axis=0)
    second = jnp.concatenate(
        [pick(w_gate), pick(w_up), down_own.reshape(part, local)], axis=1
    )
    second, _ = lax.optimization_barrier((second, first_all))
    second_all = lax.all_gather(second, "fsdp", axis=0, tiled=True)
    gate_w = second_all[:, :local]
    up_w = second_all[:, local : 2 * local]
    down_w = second_all[:, 2 * local :].reshape(fsdp, part, local).reshape(local, width)

    token_blocks = gather_blocks(tokens, seq)
    inputs_all = in_order(token_blocks, own, seq)
    cotangent_in, _ = lax.optimization_barrier((cotangent, inputs_all))
    cot_blocks = gather_blocks(cotangent_in, seq)
    cot_all = jnp.concatenate(
        [cot_blocks[at].reshape(batch * rows, width) for at in range(seq)], axis=0
    )
    out_w = lax.all_to_all(out_cols, "seq", split_axis=0, concat_axis=1, tiled=True)

    inputs_all32 = inputs_all.astype(f32)
    scale_all = rms_scale(inputs_all32)
    hat_all = inputs_all32 * scale_all
    normed = (hat_all * attn_full).astype(bf16)
    flat_normed = normed.reshape(count, width)
    qkv_raw = dot(flat_normed, w_qkv).reshape(batch, length, qkv_width)
    query_raw = qkv_raw[..., :q_width]
    key_raw = qkv_raw[..., q_width : q_width + kv_width]
    value_raw = qkv_raw[..., q_width + kv_width :]
    cosine, sine = rope_tables(jnp.arange(length, dtype=jnp.int32), HD)
    query_gain = qk_gain[0].astype(f32)
    key_gain = qk_gain[1].astype(f32)
    query_turned, query_scale = head_rope(query_raw, query_gain, cosine, sine)
    key_turned, key_scale = head_rope(key_raw, key_gain, cosine, sine)
    mixed, log_sums, query_low, key_low, value_low = attend(
        (query_turned.astype(bf16), key_turned.astype(bf16), value_raw.astype(bf16))
    )
    flat_mixed = mixed.reshape(count, q_width)
    branch = dot(flat_mixed, out_w).astype(bf16).reshape(batch, length, width)
    inputs = tokens.astype(f32)
    middle = inputs + scatter_blocks(from_order(branch, own, seq), seq)

    scale_two = rms_scale(middle)
    normed_two = (middle * scale_two * ffn_full).astype(bf16)
    two_blocks = gather_blocks(normed_two, seq)
    two_all = jnp.concatenate(
        [two_blocks[at].reshape(batch * rows, width) for at in range(seq)], axis=0
    )
    gate = dot(two_all, gate_w)
    upward = dot(two_all, up_w)
    grad_hidden = dot_t(cot_all, down_w)
    sigma = jax.nn.sigmoid(gate)
    activated = gate * sigma
    hidden = (activated * upward).astype(bf16)
    grad_gate_act = (grad_hidden * upward * sigma * (1.0 + gate * (1.0 - sigma))).astype(bf16)
    grad_upward = (grad_hidden * activated).astype(bf16)
    two_back = (dot_t(grad_gate_act, gate_w) + dot_t(grad_upward, up_w)).astype(bf16)

    def xor_blocks(flat):
        shaped = flat.reshape(seq, batch, rows, width)
        return {at: shaped[at] for at in range(seq)}

    grad_two = scatter_blocks(xor_blocks(two_back), seq)
    grad_middle_norm, grad_ffn_gain = norm_back(grad_two, middle, scale_two, ffn_full)
    grad_middle = cotangent.astype(f32) + grad_middle_norm
    grad_branch = grad_middle.astype(bf16)
    branch_blocks = gather_blocks(grad_branch, seq)
    grad_down = t_dot(hidden, cot_all).astype(bf16)
    grad_gate = t_dot(two_all, grad_gate_act).astype(bf16)
    grad_up = t_dot(two_all, grad_upward).astype(bf16)
    ffn_sums = jnp.concatenate(
        [grad_gate, grad_up, grad_down.reshape(fsdp, units, width).reshape(width, local)], axis=1
    )
    ffn_share = lax.psum_scatter(ffn_sums, "fsdp", scatter_dimension=0, tiled=True)
    result_part = dot(hidden, down_w).astype(bf16)
    result_part, _ = lax.optimization_barrier((result_part, tuple(branch_blocks.values())))
    result = (middle + scatter_blocks(xor_blocks(result_part), seq)).astype(bf16)

    branch_all = in_order(branch_blocks, own, seq).reshape(count, width)
    grad_out = t_dot(flat_mixed, branch_all).astype(bf16)
    grad_out_cols = lax.all_to_all(grad_out, "seq", split_axis=1, concat_axis=0, tiled=True)
    grad_mixed = dot_t(branch_all, out_w).astype(bf16).reshape(batch, length, q_width)
    grad_query_low, grad_key_low, grad_value_low = attend_back(
        query_low, key_low, value_low, log_sums, grad_mixed
    )
    grad_query_raw, grad_query_gain = head_rope_back(
        grad_query_low.astype(f32), query_raw, query_scale, query_gain, cosine, sine
    )
    grad_key_raw, grad_key_gain = head_rope_back(
        grad_key_low.astype(f32), key_raw, key_scale, key_gain, cosine, sine
    )
    grad_qkv = jnp.concatenate(
        [grad_query_raw.astype(bf16), grad_key_raw.astype(bf16), grad_value_low], axis=2
    ).reshape(count, qkv_width)
    normed_back = dot_t(grad_qkv, w_qkv)
    normed_back_low = normed_back.astype(bf16).reshape(batch, length, width)
    grad_attn_gain = jnp.sum(normed_back * hat_all.reshape(count, width), axis=0)
    grad_normed = scatter_blocks(from_order(normed_back_low, own, seq), seq)
    inputs_norm, _ = norm_back(grad_normed, inputs, rms_scale(inputs), attn_full)
    grad_tokens = grad_middle + inputs_norm

    gain_cols = jnp.stack([grad_attn_gain, jnp.sum(grad_ffn_gain.reshape(1, width), axis=0)], axis=1)
    last = jnp.concatenate(
        [
            t_dot(flat_normed, grad_qkv).astype(bf16),
            grad_out_cols,
            jnp.pad(gain_cols.astype(bf16), ((0, 0), (0, 126))),
        ],
        axis=1,
    )
    last_width = last.shape[1]
    qk_row = jnp.concatenate([grad_query_gain, grad_key_gain]).astype(bf16)
    qk_rows = jnp.zeros((fsdp, 16, last_width), bf16)
    qk_rows = qk_rows.at[:, 0, : 2 * HD].set(qk_row)
    last = jnp.concatenate([last.reshape(fsdp, part, last_width), qk_rows], axis=1)
    last_share = lax.psum_scatter(
        last.reshape(fsdp * (part + 16), last_width), "fsdp", scatter_dimension=0, tiled=True
    )
    ffn_shares = lax.all_gather(ffn_share, "seq", axis=0, tiled=False).astype(f32)
    last_shares = lax.all_gather(last_share, "seq", axis=0, tiled=False).astype(f32)

    def unpick(piece):
        split = piece.reshape(seq, part, fsdp, units)
        return jnp.transpose(split, (1, 2, 0, 3)).reshape(part, fsdp * seq * units)

    def side_by_side(piece):
        return jnp.transpose(piece, (1, 0, 2)).reshape(part, -1)

    shard_gate = unpick(ffn_shares[:, :, :local])
    shard_up = unpick(ffn_shares[:, :, local : 2 * local])
    shard_down = ffn_shares[:, :, 2 * local :].reshape(seq * units, width)
    top = last_shares[:, :part]
    shard_query = side_by_side(top[:, :, :q_width])
    shard_key = side_by_side(top[:, :, q_width : q_width + kv_width])
    shard_value = side_by_side(top[:, :, q_width + kv_width : qkv_width])
    shard_out = side_by_side(top[:, :, qkv_width : qkv_width + o_width])
    shard_gains = jnp.sum(top[:, :, qkv_width + o_width : qkv_width + o_width + 2], axis=0)
    gain_total = jnp.sum(last_shares[:, part, : 2 * HD], axis=0).reshape(2, HD)
    return (
        result,
        grad_tokens,
        shard_query,
        shard_key,
        shard_value,
        shard_out,
        shard_gate,
        shard_up,
        shard_down,
        shard_gains[:, 0],
        shard_gains[:, 1],
        gain_total,
    )


def solution(mesh):
    placed = (
        P("fsdp", "seq", None),
        P("fsdp", None),
        P("fsdp", None),
        P("fsdp", None),
        P("fsdp", None),
        P("fsdp", None),
        P("fsdp", None),
        P("fsdp", None),
        P("fsdp"),
        P("fsdp"),
        P(),
        P("fsdp", "seq", None),
    )
    return jax.shard_map(
        functools.partial(per_device, mesh.shape["fsdp"], mesh.shape["seq"]),
        mesh=mesh,
        in_specs=placed,
        out_specs=(
            P("fsdp", "seq", None),
            P("fsdp", "seq", None),
            P("fsdp", None),
            P("fsdp", None),
            P("fsdp", None),
            P("fsdp", None),
            P("fsdp", None),
            P("fsdp", None),
            P("fsdp", None),
            P("fsdp"),
            P("fsdp"),
            P(),
        ),
        check_vma=False,
    )
```

```python
import functools

import jax
import jax.numpy as jnp
from jax import lax
from jax.experimental import pallas as pl
from jax.experimental.pallas import tpu as pltpu
from jax.sharding import PartitionSpec as P

HD = 64


RMS_EPSILON = 1e-05
ROPE_THETA = 1000000.0


def rms_scale(values):
    return lax.rsqrt(jnp.mean(values * values, axis=-1, keepdims=True) + RMS_EPSILON)


def rope_tables(positions, head_size):
    half_size = head_size // 2
    freqs = ROPE_THETA ** (-(jnp.arange(half_size, dtype=jnp.float32) * 2.0) / head_size)
    angles = positions.astype(jnp.float32)[:, None] * freqs[None, :]
    angles = jnp.concatenate([angles, angles], axis=-1)
    return (jnp.cos(angles), jnp.sin(angles))


def norm_back(grad, values, scale, gain):
    weighted = grad * gain
    grad_values = scale * weighted - values * scale**3 * jnp.mean(
        weighted * values, axis=-1, keepdims=True
    )
    grad_gain = jnp.sum(grad * values * scale, axis=(0, 1))
    return (grad_values, grad_gain)


LANES = 128
BLOCK_ROWS = 256


def low_half(shape):
    return lax.broadcasted_iota(jnp.int32, shape, len(shape) - 1) % LANES < HD


def first_part(shape):
    return lax.broadcasted_iota(jnp.int32, shape, len(shape) - 1) % HD < HD // 2


def pair_scale(raw):
    squares = raw * raw
    low = low_half(raw.shape)
    one = jnp.sum(jnp.where(low, squares, 0.0), axis=1, keepdims=True)
    two = jnp.sum(jnp.where(low, 0.0, squares), axis=1, keepdims=True)
    one = lax.rsqrt(one * (1.0 / HD) + RMS_EPSILON)
    two = lax.rsqrt(two * (1.0 / HD) + RMS_EPSILON)
    return jnp.where(low, one, two)


def pair_turn(raw, gain, cosine, sine):
    normed = raw * pair_scale(raw) * gain
    half = HD // 2
    turned = jnp.where(
        first_part(raw.shape),
        -pltpu.roll(normed, LANES - half, 1),
        pltpu.roll(normed, half, 1),
    )
    return normed * cosine + turned * sine


def pair_turn_back(grad, raw, gain, cosine, sine):
    half = HD // 2
    crossed = grad * sine
    turned = jnp.where(
        first_part(raw.shape),
        pltpu.roll(crossed, LANES - half, 1),
        -pltpu.roll(crossed, half, 1),
    )
    grad_normed = grad * cosine + turned
    scale = pair_scale(raw)
    grad_gain = jnp.sum(grad_normed * raw * scale, axis=0, keepdims=True)
    weighted = grad_normed * gain
    product = weighted * raw
    low = low_half(raw.shape)
    one = jnp.sum(jnp.where(low, product, 0.0), axis=1, keepdims=True) * (1.0 / HD)
    two = jnp.sum(jnp.where(low, 0.0, product), axis=1, keepdims=True) * (1.0 / HD)
    mean = jnp.where(low, one, two)
    return scale * weighted - raw * (scale * scale * scale) * mean, grad_gain


def both_halves(values, group):
    mine = low_half(values.shape) == (group == 0)
    return jnp.where(mine, values, pltpu.roll(values, HD, 1))


def stack_pair(block):
    low = low_half(block.shape)
    return jnp.concatenate([jnp.where(low, block, 0.0), jnp.where(low, 0.0, block)], axis=0)


def mul(left, right, left_dim, right_dim):
    return lax.dot_general(
        left, right, (((left_dim,), (right_dim,)), ((), ())), preferred_element_type=jnp.float32
    )


def unstack_pair(turned):
    rows = turned.shape[1] // 2
    top = lax.broadcasted_iota(jnp.int32, (LANES, rows), 0) < HD
    return jnp.where(top, turned[:, :rows], turned[:, rows:]).T


def causal_block(rows):
    keys = lax.broadcasted_iota(jnp.int32, (rows, 2 * rows), 0)
    queries = lax.broadcasted_iota(jnp.int32, (rows, 2 * rows), 1) % rows
    return keys <= queries


def attend_kernel(
    q_ref, k_ref, v_ref, cos_ref, sin_ref, gain_ref, q_out, k_out, mixed_out, both_k, both_v
):
    group = pl.program_id(1)
    length = q_ref.shape[1]
    rows = min(BLOCK_ROWS, length)
    cosine = cos_ref[...]
    sine = sin_ref[...]
    queries = pair_turn(q_ref[0], gain_ref[0:1, :], cosine, sine).astype(jnp.bfloat16)
    keys = pair_turn(k_ref[0], gain_ref[1:2, :], cosine, sine).astype(jnp.bfloat16)
    q_out[0] = queries
    k_out[0] = keys
    both_k[...] = both_halves(keys.astype(jnp.float32), group).astype(jnp.bfloat16)
    both_v[...] = both_halves(v_ref[0], group).T.astype(jnp.bfloat16)
    diagonal = causal_block(rows)
    for at in range(length // rows):
        start = at * rows
        block = q_out[0, start : start + rows, :].astype(jnp.float32) * HD ** (-0.5)
        pair = stack_pair(block).astype(jnp.bfloat16)
        last = jnp.exp(mul(both_k[start : start + rows, :], pair, 1, 1))
        last = jnp.where(diagonal, last, 0.0)
        total = jnp.sum(last, axis=0, keepdims=True)
        mixed = mul(both_v[:, start : start + rows], last.astype(jnp.bfloat16), 1, 0)
        if at > 0:
            before = jnp.exp(mul(both_k[:start, :], pair, 1, 1))
            total = total + jnp.sum(before, axis=0, keepdims=True)
            mixed = mixed + mul(both_v[:, :start], before.astype(jnp.bfloat16), 1, 0)
        mixed = mixed / total
        mixed_out[0, start : start + rows, :] = unstack_pair(mixed).astype(jnp.bfloat16)


def attend_back_kernel(
    low_q_ref,
    low_k_ref,
    q_ref,
    k_ref,
    v_ref,
    grad_ref,
    cos_ref,
    sin_ref,
    gain_ref,
    grad_out,
    gain_out,
    both_k,
    both_k_turned,
    both_v,
    sum_k,
    sum_v,
    grad_q,
    kept_k,
    kept_v,
):
    group = pl.program_id(1)
    length = q_ref.shape[1]
    rows = min(BLOCK_ROWS, length)
    q_width = grad_out.shape[2] - 2 * LANES
    groups = q_width // LANES
    keys = both_halves(low_k_ref[0].astype(jnp.float32), group)
    both_k[...] = keys.astype(jnp.bfloat16)
    both_k_turned[...] = keys.T.astype(jnp.bfloat16)
    both_v[...] = both_halves(v_ref[0], group).astype(jnp.bfloat16)
    diagonal = causal_block(rows)
    head_scale = HD ** (-0.5)

    for at in range(length // rows):
        start = at * rows
        here = slice(start, start + rows)
        block = low_q_ref[0, here, :].astype(jnp.float32) * head_scale
        pair = stack_pair(block).astype(jnp.bfloat16)
        grad_pair = stack_pair(grad_ref[0, here, :].astype(jnp.float32)).astype(jnp.bfloat16)
        spans = [(here, True)] + ([(slice(0, start), False)] if at > 0 else [])
        parts = []
        total = 0.0
        for span, masked in spans:
            exps = jnp.exp(mul(both_k[span, :], pair, 1, 1))
            if masked:
                exps = jnp.where(diagonal, exps, 0.0)
            total = total + jnp.sum(exps, axis=0, keepdims=True)
            parts.append(exps)
        inverse = 1.0 / total
        inner = 0.0
        both = []
        for (span, masked), exps in zip(spans, parts):
            probs = exps * inverse
            grad_probs = mul(both_v[span, :], grad_pair, 1, 1)
            inner = inner + jnp.sum(probs * grad_probs, axis=0, keepdims=True)
            both.append((probs, grad_probs))
        turned = 0.0
        for (span, masked), (probs, grad_probs) in zip(spans, both):
            grad_scores = (probs * (grad_probs - inner)).astype(jnp.bfloat16)
            add_v = mul(probs.astype(jnp.bfloat16), grad_pair, 1, 0)
            add_k = mul(grad_scores, pair, 1, 0)
            if masked:
                sum_v[span, :] = add_v
                sum_k[span, :] = add_k
            else:
                sum_v[span, :] = sum_v[span, :] + add_v
                sum_k[span, :] = sum_k[span, :] + add_k
            turned = turned + mul(both_k_turned[:, span], grad_scores, 1, 0)
        grad_q[here, :] = unstack_pair(turned) * head_scale

    def low(values):
        return values.astype(jnp.bfloat16).astype(jnp.float32)

    cosine = cos_ref[...]
    sine = sin_ref[...]
    raw_grad, gain_grad = pair_turn_back(
        low(grad_q[...]), q_ref[0], gain_ref[0:1, :], cosine, sine
    )
    grad_out[0, :, pl.ds(pl.multiple_of(group * LANES, LANES), LANES)] = raw_grad.astype(
        jnp.bfloat16
    )

    @pl.when((group == 0) & (pl.program_id(0) == 0))
    def _():
        gain_out[...] = jnp.zeros_like(gain_out)

    gain_out[0:1, :] = gain_out[0:1, :] + gain_grad
    mine = low_half((length, LANES)) == (group == 0)
    whole_k = sum_k[...] + pltpu.roll(sum_k[...], HD, 1)
    whole_v = sum_v[...] + pltpu.roll(sum_v[...], HD, 1)

    @pl.when(group == 0)
    def _():
        kept_k[...] = whole_k
        kept_v[...] = whole_v

    @pl.when(group == groups - 1)
    def _():
        all_k = low(jnp.where(mine, whole_k, kept_k[...]))
        all_v = jnp.where(mine, whole_v, kept_v[...])
        raw_k, gain_k = pair_turn_back(all_k, k_ref[0], gain_ref[1:2, :], cosine, sine)
        grad_out[0, :, q_width : q_width + LANES] = raw_k.astype(jnp.bfloat16)
        grad_out[0, :, q_width + LANES :] = all_v.astype(jnp.bfloat16)
        gain_out[1:2, :] = gain_out[1:2, :] + gain_k


def head_tables(length, qk_gain):
    cosine, sine = rope_tables(jnp.arange(length, dtype=jnp.int32), HD)
    twice = lambda table: jnp.concatenate([table, table], axis=1)
    return twice(cosine), twice(sine), twice(qk_gain.astype(jnp.float32))


def attend(qkv_raw, tables):
    batch, length, width = qkv_raw.shape
    groups = width // LANES - 2
    assert groups == 2
    column = lambda at: pl.BlockSpec((1, length, LANES), lambda b, g: (b, 0, at))
    own_column = pl.BlockSpec((1, length, LANES), lambda b, g: (b, 0, g))
    table = pl.BlockSpec((length, LANES), lambda b, g: (0, 0))
    pairs = batch * groups * length * length
    return pl.pallas_call(
        attend_kernel,
        grid=(batch, groups),
        in_specs=[
            own_column,
            column(groups),
            column(groups + 1),
            table,
            table,
            pl.BlockSpec((2, LANES), lambda b, g: (0, 0)),
        ],
        out_specs=[own_column, column(0), own_column],
        out_shape=[
            jax.ShapeDtypeStruct((batch, length, groups * LANES), jnp.bfloat16),
            jax.ShapeDtypeStruct((batch, length, LANES), jnp.bfloat16),
            jax.ShapeDtypeStruct((batch, length, groups * LANES), jnp.bfloat16),
        ],
        scratch_shapes=[
            pltpu.VMEM((length, LANES), jnp.bfloat16),
            pltpu.VMEM((LANES, length), jnp.bfloat16),
        ],
        cost_estimate=pl.CostEstimate(
            flops=pairs * 512, transcendentals=pairs, bytes_accessed=8 * qkv_raw.size
        ),
        name="attend",
    )(qkv_raw, qkv_raw, qkv_raw, *tables)


def attend_back(query_low, key_low, qkv_raw, grad_mixed, tables):
    batch, length, width = qkv_raw.shape
    groups = width // LANES - 2
    column = lambda at: pl.BlockSpec((1, length, LANES), lambda b, g: (b, 0, at))
    own_column = pl.BlockSpec((1, length, LANES), lambda b, g: (b, 0, g))
    table = pl.BlockSpec((length, LANES), lambda b, g: (0, 0))
    pairs = batch * groups * length * length
    return pl.pallas_call(
        attend_back_kernel,
        grid=(batch, groups),
        in_specs=[
            own_column,
            column(0),
            own_column,
            column(groups),
            column(groups + 1),
            own_column,
            table,
            table,
            pl.BlockSpec((2, LANES), lambda b, g: (0, 0)),
        ],
        out_specs=[
            pl.BlockSpec((1, length, width), lambda b, g: (b, 0, 0)),
            pl.BlockSpec((8, LANES), lambda b, g: (0, 0)),
        ],
        out_shape=[
            jax.ShapeDtypeStruct((batch, length, width), jnp.bfloat16),
            jax.ShapeDtypeStruct((8, LANES), jnp.float32),
        ],
        scratch_shapes=[
            pltpu.VMEM((length, LANES), jnp.bfloat16),
            pltpu.VMEM((LANES, length), jnp.bfloat16),
            pltpu.VMEM((length, LANES), jnp.bfloat16),
        ]
        + [pltpu.VMEM((length, LANES), jnp.float32)] * 5,
        cost_estimate=pl.CostEstimate(
            flops=pairs * 1280, transcendentals=pairs, bytes_accessed=12 * qkv_raw.size
        ),
        name="attend_back",
    )(query_low, key_low, qkv_raw, qkv_raw, qkv_raw, grad_mixed, *tables)


FFN_ROWS = 256


def ffn_kernel(two_ref, cot_ref, gate_w, up_w, down_w, *refs):
    hidden_out, gate_out, up_out, result_out, back_out = refs[-5:]
    two = two_ref[...]
    gate = mul(two, gate_w[...], 1, 0)
    upward = mul(two, up_w[...], 1, 0)
    grad_hidden = mul(cot_ref[...], down_w[...], 1, 1)
    sigma = 1.0 / (1.0 + jnp.exp(-gate))
    activated = gate * sigma
    hidden = (activated * upward).astype(jnp.bfloat16)
    grad_gate = grad_hidden * upward * sigma * (1.0 + gate * (1.0 - sigma))
    grad_gate = grad_gate.astype(jnp.bfloat16)
    grad_up = (grad_hidden * activated).astype(jnp.bfloat16)
    hidden_out[...] = hidden
    gate_out[...] = grad_gate
    up_out[...] = grad_up
    result_out[...] = mul(hidden, down_w[...], 1, 0).astype(jnp.bfloat16)
    back = mul(grad_gate, gate_w[...], 1, 1) + mul(grad_up, up_w[...], 1, 1)
    back_out[...] = back.astype(jnp.bfloat16)


def ffn(two, cot_all, second_all, down_w, first_row, kept):
    rows, width = two.shape
    local = down_w.shape[0]
    step = min(FFN_ROWS, rows)
    offset = first_row // step
    here = lambda size: pl.BlockSpec((step, size), lambda i: (i, 0))
    there = lambda size: pl.BlockSpec((step, size), lambda i: (i + offset, 0))
    whole = lambda shape, at: pl.BlockSpec(shape, lambda i: (0, at))
    total = cot_all.shape[0]
    kept = () if kept is None else kept
    return pl.pallas_call(
        ffn_kernel,
        grid=(rows // step,),
        in_specs=[
            here(width),
            there(width),
            whole((width, local), 0),
            whole((width, local), 1),
            whole((local, width), 0),
        ]
        + [pl.BlockSpec(memory_space=pl.ANY)] * len(kept),
        out_specs=[there(local)] * 3 + [here(width)] * 2,
        out_shape=[jax.ShapeDtypeStruct((total, local), jnp.bfloat16)] * 3
        + [jax.ShapeDtypeStruct((rows, width), jnp.bfloat16)] * 2,
        input_output_aliases={5 + at: at for at in range(len(kept))},
        cost_estimate=pl.CostEstimate(
            flops=12 * rows * width * local,
            transcendentals=rows * local,
            bytes_accessed=2 * (3 * width * local + rows * (4 * width + 3 * local)),
        ),
        name="ffn",
    )(two, cot_all, second_all, second_all, down_w, *kept)


def fold_rows(piece, part):
    units, width = piece.shape
    extra = piece[part:].reshape(units - part, width // LANES, LANES)
    extra = jnp.transpose(extra, (1, 0, 2)).reshape(part, LANES)
    return jnp.concatenate([piece[:part], extra], axis=1)


def unfold_rows(folded, units):
    lead = folded.shape[:-2]
    part = folded.shape[-2]
    width = folded.shape[-1] - LANES
    extra = folded[..., width:].reshape(lead + (width // LANES, units - part, LANES))
    extra = jnp.swapaxes(extra, -3, -2).reshape(lead + (units - part, width))
    return jnp.concatenate([folded[..., :width], extra], axis=-2)


def bits_of(count):
    return [1 << i for i in range(count.bit_length() - 1)]


def swap(values, bit, count):
    return lax.ppermute(values, "seq", [(i, i ^ bit) for i in range(count)])


def gather_blocks(block, count):
    blocks = {0: block}
    for bit in reversed(bits_of(count)):
        for at in list(blocks):
            blocks[at | bit] = swap(blocks[at], bit, count)
    return blocks


def scatter_blocks(blocks, count):
    blocks = dict(blocks)
    for bit in bits_of(count):
        kept = {}
        for at in blocks:
            if not at & bit:
                arrived = swap(blocks[at | bit].astype(jnp.bfloat16), bit, count)
                kept[at] = blocks[at].astype(jnp.float32) + arrived.astype(jnp.float32)
        blocks = kept
    return blocks[0]


def in_order(blocks, own, count):
    batch, rows, width = blocks[0].shape
    whole = jnp.zeros((batch, count * rows, width), blocks[0].dtype)
    for at in range(count):
        whole = lax.dynamic_update_slice(whole, blocks[at], (0, (own ^ at) * rows, 0))
    return whole


def from_order(whole, own, count):
    rows = whole.shape[1] // count
    return {
        at: lax.dynamic_slice_in_dim(whole, (own ^ at) * rows, rows, axis=1) for at in range(count)
    }


def dot(left, right):
    return jnp.dot(left, right, preferred_element_type=jnp.float32)


def dot_t(left, right):
    return lax.dot_general(
        left, right, (((1,), (1,)), ((), ())), preferred_element_type=jnp.float32
    )


def t_dot(left, right):
    return lax.dot_general(
        left, right, (((0,), (0,)), ((), ())), preferred_element_type=jnp.float32
    )


def per_device(
    fsdp,
    seq,
    tokens,
    w_query,
    w_key,
    w_value,
    w_out,
    w_gate,
    w_up,
    w_down,
    attn_gain,
    ffn_gain,
    qk_gain,
    cotangent,
):
    bf16 = jnp.bfloat16
    f32 = jnp.float32
    own = lax.axis_index("seq")
    batch, rows, width = tokens.shape
    length = rows * seq
    count = batch * length
    part = w_query.shape[0]
    q_width = w_query.shape[1] // seq
    kv_width = w_key.shape[1] // seq
    o_width = w_out.shape[1] // seq
    units = w_down.shape[0] // seq
    local = units * fsdp

    def columns(weight, size):
        return lax.dynamic_slice_in_dim(weight, own * size, size, axis=1)

    gains = jnp.stack([attn_gain, ffn_gain], axis=1)
    first = jnp.concatenate(
        [
            columns(w_query, q_width),
            columns(w_key, kv_width),
            columns(w_value, kv_width),
            columns(w_out, o_width),
            jnp.pad(gains, ((0, 0), (0, 126))),
        ],
        axis=1,
    )
    first_all = lax.all_gather(first, "fsdp", axis=0, tiled=True)
    qkv_width = q_width + 2 * kv_width
    w_qkv = first_all[:, :qkv_width]
    out_cols = first_all[:, qkv_width : qkv_width + o_width]
    attn_full = first_all[:, qkv_width + o_width].astype(f32)
    ffn_full = first_all[:, qkv_width + o_width + 1].astype(f32)

    def pick(weight):
        split = weight.reshape(part, fsdp, seq, units)
        return lax.dynamic_index_in_dim(split, own, axis=2, keepdims=False).reshape(part, local)

    down_own = lax.dynamic_slice_in_dim(w_down, own * units, units, axis=0)
    second = jnp.concatenate(
        [pick(w_gate), pick(w_up), fold_rows(down_own, part)], axis=1
    )
    second, _ = lax.optimization_barrier((second, first_all))
    second_all = lax.all_gather(second, "fsdp", axis=0, tiled=True)
    down_w = unfold_rows(second_all[:, 2 * local :].reshape(fsdp, part, local), units)
    down_w = down_w.reshape(local, width)

    token_blocks = gather_blocks(tokens, seq)
    inputs_all = in_order(token_blocks, own, seq)
    cotangent_in, _ = lax.optimization_barrier((cotangent, inputs_all))
    cot_blocks = gather_blocks(cotangent_in, seq)
    cot_all = jnp.concatenate(
        [cot_blocks[at].reshape(batch * rows, width) for at in range(seq)], axis=0
    )
    out_w = lax.all_to_all(out_cols, "seq", split_axis=0, concat_axis=1, tiled=True)

    inputs_all32 = inputs_all.astype(f32)
    scale_all = rms_scale(inputs_all32)
    hat_all = inputs_all32 * scale_all
    normed = (hat_all * attn_full).astype(bf16)
    flat_normed = normed.reshape(count, width)
    qkv_raw = dot(flat_normed, w_qkv).reshape(batch, length, qkv_width)
    tables = head_tables(length, qk_gain)
    query_low, key_low, mixed = attend(qkv_raw, tables)
    flat_mixed = mixed.reshape(count, q_width)
    branch = dot(flat_mixed, out_w).astype(bf16).reshape(batch, length, width)
    branch, cot_all = lax.optimization_barrier((branch, cot_all))
    inputs = tokens.astype(f32)
    middle = inputs + scatter_blocks(from_order(branch, own, seq), seq)

    scale_two = rms_scale(middle)
    normed_two = (middle * scale_two * ffn_full).astype(bf16)
    two_blocks = gather_blocks(normed_two, seq)
    flat = lambda values: values.reshape(batch * rows, width)
    half = seq // 2
    near = jnp.concatenate([flat(two_blocks[at]) for at in range(half)], axis=0)
    *kept, result_near, back_near = ffn(near, cot_all, second_all, down_w, 0, None)
    far = jnp.concatenate([flat(two_blocks[at]) for at in range(half, seq)], axis=0)
    hidden, grad_gate_act, grad_upward, result_far, back_far = ffn(
        far, cot_all, second_all, down_w, half * batch * rows, kept
    )
    two_all = jnp.concatenate([near, far], axis=0)

    def xor_blocks(one, two):
        pieces = [values.reshape(half, batch, rows, width) for values in (one, two)]
        return {at: pieces[at // half][at % half] for at in range(seq)}

    grad_two = scatter_blocks(xor_blocks(back_near, back_far), seq)
    grad_middle_norm, grad_ffn_gain = norm_back(grad_two, middle, scale_two, ffn_full)
    grad_middle = cotangent.astype(f32) + grad_middle_norm
    grad_branch = grad_middle.astype(bf16)
    branch_blocks = gather_blocks(grad_branch, seq)
    grad_down = t_dot(hidden, cot_all).astype(bf16)
    grad_gate = t_dot(two_all, grad_gate_act).astype(bf16)
    grad_up = t_dot(two_all, grad_upward).astype(bf16)
    grad_down = jax.vmap(lambda piece: fold_rows(piece, part))(grad_down.reshape(fsdp, units, width))
    grad_down = grad_down.reshape(width, local)
    ffn_sums = jnp.concatenate(
        [grad_gate, grad_up, grad_down], axis=1
    )
    ffn_share = lax.psum_scatter(ffn_sums, "fsdp", scatter_dimension=0, tiled=True)
    result_parts, _ = lax.optimization_barrier(
        ((result_near, result_far), tuple(branch_blocks.values()))
    )
    result = (middle + scatter_blocks(xor_blocks(*result_parts), seq)).astype(bf16)

    branch_all = in_order(branch_blocks, own, seq).reshape(count, width)
    grad_out = t_dot(flat_mixed, branch_all).astype(bf16)
    grad_out_cols = lax.all_to_all(grad_out, "seq", split_axis=1, concat_axis=0, tiled=True)
    grad_mixed = dot_t(branch_all, out_w).astype(bf16).reshape(batch, length, q_width)
    grad_qkv, gain_sums = attend_back(query_low, key_low, qkv_raw, grad_mixed, tables)
    grad_qkv, result = lax.optimization_barrier((grad_qkv, result))
    grad_qkv = grad_qkv.reshape(count, qkv_width)
    normed_back = dot_t(grad_qkv, w_qkv)
    normed_back_low = normed_back.astype(bf16).reshape(batch, length, width)
    grad_attn_gain = jnp.sum(normed_back * hat_all.reshape(count, width), axis=0)
    grad_normed = scatter_blocks(from_order(normed_back_low, own, seq), seq)
    inputs_norm, _ = norm_back(grad_normed, inputs, rms_scale(inputs), attn_full)
    grad_tokens = grad_middle + inputs_norm

    gain_cols = jnp.stack([grad_attn_gain, jnp.sum(grad_ffn_gain.reshape(1, width), axis=0)], axis=1)
    last = jnp.concatenate(
        [
            t_dot(flat_normed, grad_qkv).astype(bf16),
            grad_out_cols,
            jnp.pad(gain_cols.astype(bf16), ((0, 0), (0, 126))),
        ],
        axis=1,
    )
    last_width = last.shape[1]
    gain_sums = gain_sums[:2, :HD] + gain_sums[:2, HD:]
    qk_row = gain_sums.reshape(2 * HD).astype(bf16)
    qk_rows = jnp.zeros((fsdp, 16, last_width), bf16)
    qk_rows = qk_rows.at[:, 0, : 2 * HD].set(qk_row)
    last = jnp.concatenate([last.reshape(fsdp, part, last_width), qk_rows], axis=1)
    last_share = lax.psum_scatter(
        last.reshape(fsdp * (part + 16), last_width), "fsdp", scatter_dimension=0, tiled=True
    )
    share_blocks = gather_blocks(ffn_share, seq)
    ffn_shares = jnp.stack([share_blocks[at] for at in range(seq)]).astype(f32)
    for bit in bits_of(seq):
        turned = ffn_shares.reshape(-1, 2, bit, part, ffn_share.shape[1])[:, ::-1]
        ffn_shares = jnp.where((own & bit) > 0, turned.reshape(ffn_shares.shape), ffn_shares)
    last_shares = lax.all_gather(last_share, "seq", axis=0, tiled=False).astype(f32)

    def unpick(piece):
        split = piece.reshape(seq, part, fsdp, units)
        return jnp.transpose(split, (1, 2, 0, 3)).reshape(part, fsdp * seq * units)

    def side_by_side(piece):
        return jnp.transpose(piece, (1, 0, 2)).reshape(part, -1)

    shard_gate = unpick(ffn_shares[:, :, :local])
    shard_up = unpick(ffn_shares[:, :, local : 2 * local])
    shard_down = unfold_rows(ffn_shares[:, :, 2 * local :], units).reshape(seq * units, width)
    top = last_shares[:, :part]
    shard_query = side_by_side(top[:, :, :q_width])
    shard_key = side_by_side(top[:, :, q_width : q_width + kv_width])
    shard_value = side_by_side(top[:, :, q_width + kv_width : qkv_width])
    shard_out = side_by_side(top[:, :, qkv_width : qkv_width + o_width])
    shard_gains = jnp.sum(top[:, :, qkv_width + o_width : qkv_width + o_width + 2], axis=0)
    gain_total = jnp.sum(last_shares[:, part, : 2 * HD], axis=0).reshape(2, HD)
    return (
        result,
        grad_tokens,
        shard_query,
        shard_key,
        shard_value,
        shard_out,
        shard_gate,
        shard_up,
        shard_down,
        shard_gains[:, 0],
        shard_gains[:, 1],
        gain_total,
    )


def solution(mesh):
    placed = (
        P("fsdp", "seq", None),
        P("fsdp", None),
        P("fsdp", None),
        P("fsdp", None),
        P("fsdp", None),
        P("fsdp", None),
        P("fsdp", None),
        P("fsdp", None),
        P("fsdp"),
        P("fsdp"),
        P(),
        P("fsdp", "seq", None),
    )
    return jax.shard_map(
        functools.partial(per_device, mesh.shape["fsdp"], mesh.shape["seq"]),
        mesh=mesh,
        in_specs=placed,
        out_specs=(
            P("fsdp", "seq", None),
            P("fsdp", "seq", None),
            P("fsdp", None),
            P("fsdp", None),
            P("fsdp", None),
            P("fsdp", None),
            P("fsdp", None),
            P("fsdp", None),
            P("fsdp", None),
            P("fsdp"),
            P("fsdp"),
            P(),
        ),
        check_vma=False,
    )
```

```python
import functools

import jax
import jax.numpy as jnp
from jax import lax
from jax.experimental import pallas as pl
from jax.experimental.pallas import tpu as pltpu
from jax.sharding import PartitionSpec as P

HD = 64


RMS_EPSILON = 1e-05
ROPE_THETA = 1000000.0


def rms_scale(values):
    return lax.rsqrt(jnp.mean(values * values, axis=-1, keepdims=True) + RMS_EPSILON)


def rope_tables(positions, head_size):
    half_size = head_size // 2
    freqs = ROPE_THETA ** (-(jnp.arange(half_size, dtype=jnp.float32) * 2.0) / head_size)
    angles = positions.astype(jnp.float32)[:, None] * freqs[None, :]
    angles = jnp.concatenate([angles, angles], axis=-1)
    return (jnp.cos(angles), jnp.sin(angles))


def norm_back(grad, values, scale, gain):
    weighted = grad * gain
    grad_values = scale * weighted - values * scale**3 * jnp.mean(
        weighted * values, axis=-1, keepdims=True
    )
    grad_gain = jnp.sum(grad * values * scale, axis=(0, 1))
    return (grad_values, grad_gain)


LANES = 128
BLOCK_ROWS = 256


def low_half(shape):
    return lax.broadcasted_iota(jnp.int32, shape, len(shape) - 1) % LANES < HD


def first_part(shape):
    return lax.broadcasted_iota(jnp.int32, shape, len(shape) - 1) % HD < HD // 2


def pair_scale(raw):
    squares = raw * raw
    low = low_half(raw.shape)
    one = jnp.sum(jnp.where(low, squares, 0.0), axis=1, keepdims=True)
    two = jnp.sum(jnp.where(low, 0.0, squares), axis=1, keepdims=True)
    one = lax.rsqrt(one * (1.0 / HD) + RMS_EPSILON)
    two = lax.rsqrt(two * (1.0 / HD) + RMS_EPSILON)
    return jnp.where(low, one, two)


def pair_turn(raw, gain, cosine, sine):
    normed = raw * pair_scale(raw) * gain
    half = HD // 2
    turned = jnp.where(
        first_part(raw.shape),
        -pltpu.roll(normed, LANES - half, 1),
        pltpu.roll(normed, half, 1),
    )
    return normed * cosine + turned * sine


def pair_turn_back(grad, raw, gain, cosine, sine):
    half = HD // 2
    crossed = grad * sine
    turned = jnp.where(
        first_part(raw.shape),
        pltpu.roll(crossed, LANES - half, 1),
        -pltpu.roll(crossed, half, 1),
    )
    grad_normed = grad * cosine + turned
    scale = pair_scale(raw)
    grad_gain = jnp.sum(grad_normed * raw * scale, axis=0, keepdims=True)
    weighted = grad_normed * gain
    product = weighted * raw
    low = low_half(raw.shape)
    one = jnp.sum(jnp.where(low, product, 0.0), axis=1, keepdims=True) * (1.0 / HD)
    two = jnp.sum(jnp.where(low, 0.0, product), axis=1, keepdims=True) * (1.0 / HD)
    mean = jnp.where(low, one, two)
    return scale * weighted - raw * (scale * scale * scale) * mean, grad_gain


def both_halves(values, group):
    mine = low_half(values.shape) == (group == 0)
    return jnp.where(mine, values, pltpu.roll(values, HD, 1))


def stack_pair(block):
    low = low_half(block.shape)
    return jnp.concatenate([jnp.where(low, block, 0.0), jnp.where(low, 0.0, block)], axis=0)


def mul(left, right, left_dim, right_dim):
    return lax.dot_general(
        left, right, (((left_dim,), (right_dim,)), ((), ())), preferred_element_type=jnp.float32
    )


def unstack_pair(turned):
    rows = turned.shape[1] // 2
    top = lax.broadcasted_iota(jnp.int32, (LANES, rows), 0) < HD
    return jnp.where(top, turned[:, :rows], turned[:, rows:]).T


def causal_block(rows):
    keys = lax.broadcasted_iota(jnp.int32, (rows, 2 * rows), 0)
    queries = lax.broadcasted_iota(jnp.int32, (rows, 2 * rows), 1) % rows
    return keys <= queries


def attend_kernel(
    q_ref, k_ref, v_ref, cos_ref, sin_ref, gain_ref, q_out, k_out, mixed_out, both_k, both_v
):
    group = pl.program_id(1)
    length = q_ref.shape[1]
    rows = min(BLOCK_ROWS, length)
    cosine = cos_ref[...]
    sine = sin_ref[...]
    queries = pair_turn(q_ref[0], gain_ref[0:1, :], cosine, sine).astype(jnp.bfloat16)
    keys = pair_turn(k_ref[0], gain_ref[1:2, :], cosine, sine).astype(jnp.bfloat16)
    q_out[0] = queries
    k_out[0] = keys
    both_k[...] = both_halves(keys.astype(jnp.float32), group).astype(jnp.bfloat16)
    both_v[...] = both_halves(v_ref[0], group).T.astype(jnp.bfloat16)
    diagonal = causal_block(rows)
    for at in range(length // rows):
        start = at * rows
        block = q_out[0, start : start + rows, :].astype(jnp.float32) * HD ** (-0.5)
        pair = stack_pair(block).astype(jnp.bfloat16)
        last = jnp.exp(mul(both_k[start : start + rows, :], pair, 1, 1))
        last = jnp.where(diagonal, last, 0.0)
        total = jnp.sum(last, axis=0, keepdims=True)
        mixed = mul(both_v[:, start : start + rows], last.astype(jnp.bfloat16), 1, 0)
        if at > 0:
            before = jnp.exp(mul(both_k[:start, :], pair, 1, 1))
            total = total + jnp.sum(before, axis=0, keepdims=True)
            mixed = mixed + mul(both_v[:, :start], before.astype(jnp.bfloat16), 1, 0)
        mixed = mixed / total
        mixed_out[0, start : start + rows, :] = unstack_pair(mixed).astype(jnp.bfloat16)


def attend_back_kernel(
    low_q_ref,
    low_k_ref,
    q_ref,
    k_ref,
    v_ref,
    grad_ref,
    cos_ref,
    sin_ref,
    gain_ref,
    grad_out,
    gain_out,
    both_k,
    both_k_turned,
    both_v,
    sum_k,
    sum_v,
    grad_q,
    kept_k,
    kept_v,
):
    group = pl.program_id(1)
    length = q_ref.shape[1]
    rows = min(BLOCK_ROWS, length)
    q_width = grad_out.shape[2] - 2 * LANES
    groups = q_width // LANES
    keys = both_halves(low_k_ref[0].astype(jnp.float32), group)
    both_k[...] = keys.astype(jnp.bfloat16)
    both_k_turned[...] = keys.T.astype(jnp.bfloat16)
    both_v[...] = both_halves(v_ref[0], group).astype(jnp.bfloat16)
    diagonal = causal_block(rows)
    head_scale = HD ** (-0.5)

    for at in range(length // rows):
        start = at * rows
        here = slice(start, start + rows)
        block = low_q_ref[0, here, :].astype(jnp.float32) * head_scale
        pair = stack_pair(block).astype(jnp.bfloat16)
        grad_pair = stack_pair(grad_ref[0, here, :].astype(jnp.float32)).astype(jnp.bfloat16)
        spans = [(here, True)] + ([(slice(0, start), False)] if at > 0 else [])
        parts = []
        total = 0.0
        for span, masked in spans:
            exps = jnp.exp(mul(both_k[span, :], pair, 1, 1))
            if masked:
                exps = jnp.where(diagonal, exps, 0.0)
            total = total + jnp.sum(exps, axis=0, keepdims=True)
            parts.append(exps)
        inverse = 1.0 / total
        inner = 0.0
        both = []
        for (span, masked), exps in zip(spans, parts):
            probs = exps * inverse
            grad_probs = mul(both_v[span, :], grad_pair, 1, 1)
            inner = inner + jnp.sum(probs * grad_probs, axis=0, keepdims=True)
            both.append((probs, grad_probs))
        turned = 0.0
        for (span, masked), (probs, grad_probs) in zip(spans, both):
            grad_scores = (probs * (grad_probs - inner)).astype(jnp.bfloat16)
            add_v = mul(probs.astype(jnp.bfloat16), grad_pair, 1, 0)
            add_k = mul(grad_scores, pair, 1, 0)
            if masked:
                sum_v[span, :] = add_v
                sum_k[span, :] = add_k
            else:
                sum_v[span, :] = sum_v[span, :] + add_v
                sum_k[span, :] = sum_k[span, :] + add_k
            turned = turned + mul(both_k_turned[:, span], grad_scores, 1, 0)
        grad_q[here, :] = unstack_pair(turned) * head_scale

    def low(values):
        return values.astype(jnp.bfloat16).astype(jnp.float32)

    cosine = cos_ref[...]
    sine = sin_ref[...]
    raw_grad, gain_grad = pair_turn_back(
        low(grad_q[...]), q_ref[0], gain_ref[0:1, :], cosine, sine
    )
    grad_out[0, :, pl.ds(pl.multiple_of(group * LANES, LANES), LANES)] = raw_grad.astype(
        jnp.bfloat16
    )

    @pl.when((group == 0) & (pl.program_id(0) == 0))
    def _():
        gain_out[...] = jnp.zeros_like(gain_out)

    gain_out[0:1, :] = gain_out[0:1, :] + gain_grad
    mine = low_half((length, LANES)) == (group == 0)
    whole_k = sum_k[...] + pltpu.roll(sum_k[...], HD, 1)
    whole_v = sum_v[...] + pltpu.roll(sum_v[...], HD, 1)

    @pl.when(group == 0)
    def _():
        kept_k[...] = whole_k
        kept_v[...] = whole_v

    @pl.when(group == groups - 1)
    def _():
        all_k = low(jnp.where(mine, whole_k, kept_k[...]))
        all_v = jnp.where(mine, whole_v, kept_v[...])
        raw_k, gain_k = pair_turn_back(all_k, k_ref[0], gain_ref[1:2, :], cosine, sine)
        grad_out[0, :, q_width : q_width + LANES] = raw_k.astype(jnp.bfloat16)
        grad_out[0, :, q_width + LANES :] = all_v.astype(jnp.bfloat16)
        gain_out[1:2, :] = gain_out[1:2, :] + gain_k


def head_tables(length, qk_gain):
    cosine, sine = rope_tables(jnp.arange(length, dtype=jnp.int32), HD)
    twice = lambda table: jnp.concatenate([table, table], axis=1)
    return twice(cosine), twice(sine), twice(qk_gain.astype(jnp.float32))


def attend(qkv_raw, tables):
    batch, length, width = qkv_raw.shape
    groups = width // LANES - 2
    assert groups == 2
    column = lambda at: pl.BlockSpec((1, length, LANES), lambda b, g: (b, 0, at))
    own_column = pl.BlockSpec((1, length, LANES), lambda b, g: (b, 0, g))
    table = pl.BlockSpec((length, LANES), lambda b, g: (0, 0))
    pairs = batch * groups * length * length
    return pl.pallas_call(
        attend_kernel,
        grid=(batch, groups),
        in_specs=[
            own_column,
            column(groups),
            column(groups + 1),
            table,
            table,
            pl.BlockSpec((2, LANES), lambda b, g: (0, 0)),
        ],
        out_specs=[own_column, column(0), own_column],
        out_shape=[
            jax.ShapeDtypeStruct((batch, length, groups * LANES), jnp.bfloat16),
            jax.ShapeDtypeStruct((batch, length, LANES), jnp.bfloat16),
            jax.ShapeDtypeStruct((batch, length, groups * LANES), jnp.bfloat16),
        ],
        scratch_shapes=[
            pltpu.VMEM((length, LANES), jnp.bfloat16),
            pltpu.VMEM((LANES, length), jnp.bfloat16),
        ],
        cost_estimate=pl.CostEstimate(
            flops=pairs * 512, transcendentals=pairs, bytes_accessed=8 * qkv_raw.size
        ),
        name="attend",
    )(qkv_raw, qkv_raw, qkv_raw, *tables)


def attend_back(query_low, key_low, qkv_raw, grad_mixed, tables):
    batch, length, width = qkv_raw.shape
    groups = width // LANES - 2
    column = lambda at: pl.BlockSpec((1, length, LANES), lambda b, g: (b, 0, at))
    own_column = pl.BlockSpec((1, length, LANES), lambda b, g: (b, 0, g))
    table = pl.BlockSpec((length, LANES), lambda b, g: (0, 0))
    pairs = batch * groups * length * length
    return pl.pallas_call(
        attend_back_kernel,
        grid=(batch, groups),
        in_specs=[
            own_column,
            column(0),
            own_column,
            column(groups),
            column(groups + 1),
            own_column,
            table,
            table,
            pl.BlockSpec((2, LANES), lambda b, g: (0, 0)),
        ],
        out_specs=[
            pl.BlockSpec((1, length, width), lambda b, g: (b, 0, 0)),
            pl.BlockSpec((8, LANES), lambda b, g: (0, 0)),
        ],
        out_shape=[
            jax.ShapeDtypeStruct((batch, length, width), jnp.bfloat16),
            jax.ShapeDtypeStruct((8, LANES), jnp.float32),
        ],
        scratch_shapes=[
            pltpu.VMEM((length, LANES), jnp.bfloat16),
            pltpu.VMEM((LANES, length), jnp.bfloat16),
            pltpu.VMEM((length, LANES), jnp.bfloat16),
        ]
        + [pltpu.VMEM((length, LANES), jnp.float32)] * 5,
        cost_estimate=pl.CostEstimate(
            flops=pairs * 1280, transcendentals=pairs, bytes_accessed=12 * qkv_raw.size
        ),
        name="attend_back",
    )(query_low, key_low, qkv_raw, qkv_raw, qkv_raw, grad_mixed, *tables)


FFN_ROWS = 256


def ffn_kernel(two_ref, cot_ref, gate_w, up_w, down_w, *refs):
    hidden_out, gate_out, up_out, result_out, back_out = refs[-5:]
    two = two_ref[...]
    gate = mul(two, gate_w[...], 1, 0)
    upward = mul(two, up_w[...], 1, 0)
    grad_hidden = mul(cot_ref[...], down_w[...], 1, 1)
    sigma = 1.0 / (1.0 + jnp.exp(-gate))
    activated = gate * sigma
    hidden = (activated * upward).astype(jnp.bfloat16)
    grad_gate = grad_hidden * upward * sigma * (1.0 + gate * (1.0 - sigma))
    grad_gate = grad_gate.astype(jnp.bfloat16)
    grad_up = (grad_hidden * activated).astype(jnp.bfloat16)
    hidden_out[...] = hidden
    gate_out[...] = grad_gate
    up_out[...] = grad_up
    result_out[...] = mul(hidden, down_w[...], 1, 0).astype(jnp.bfloat16)
    back = mul(grad_gate, gate_w[...], 1, 1) + mul(grad_up, up_w[...], 1, 1)
    back_out[...] = back.astype(jnp.bfloat16)


def ffn(two, cot_all, second_all, down_w, first_row, kept):
    rows, width = two.shape
    local = down_w.shape[0]
    step = min(FFN_ROWS, rows)
    offset = first_row // step
    here = lambda size: pl.BlockSpec((step, size), lambda i: (i, 0))
    there = lambda size: pl.BlockSpec((step, size), lambda i: (i + offset, 0))
    whole = lambda shape, at: pl.BlockSpec(shape, lambda i: (0, at))
    total = cot_all.shape[0]
    kept = () if kept is None else kept
    return pl.pallas_call(
        ffn_kernel,
        grid=(rows // step,),
        in_specs=[
            here(width),
            there(width),
            whole((width, local), 0),
            whole((width, local), 1),
            whole((local, width), 0),
        ]
        + [pl.BlockSpec(memory_space=pl.ANY)] * len(kept),
        out_specs=[there(local)] * 3 + [here(width)] * 2,
        out_shape=[jax.ShapeDtypeStruct((total, local), jnp.bfloat16)] * 3
        + [jax.ShapeDtypeStruct((rows, width), jnp.bfloat16)] * 2,
        input_output_aliases={5 + at: at for at in range(len(kept))},
        cost_estimate=pl.CostEstimate(
            flops=12 * rows * width * local,
            transcendentals=rows * local,
            bytes_accessed=2 * (3 * width * local + rows * (4 * width + 3 * local)),
        ),
        name="ffn",
    )(two, cot_all, second_all, second_all, down_w, *kept)


def fold_rows(piece, part):
    units, width = piece.shape
    extra = piece[part:].reshape(units - part, width // LANES, LANES)
    extra = jnp.transpose(extra, (1, 0, 2)).reshape(part, LANES)
    return jnp.concatenate([piece[:part], extra], axis=1)


def unfold_rows(folded, units):
    lead = folded.shape[:-2]
    part = folded.shape[-2]
    width = folded.shape[-1] - LANES
    extra = folded[..., width:].reshape(lead + (width // LANES, units - part, LANES))
    extra = jnp.swapaxes(extra, -3, -2).reshape(lead + (units - part, width))
    return jnp.concatenate([folded[..., :width], extra], axis=-2)


def bits_of(count):
    return [1 << i for i in range(count.bit_length() - 1)]


def swap(values, bit, count, axis="seq"):
    total = lax.axis_size(axis)
    return lax.ppermute(values, axis, [(i, i ^ bit) for i in range(total)])


def after(value, *others):
    return lax.optimization_barrier((value, others))[0]


def gather_blocks(block, count, hold=None):
    blocks = {0: block}
    for bit in reversed(bits_of(count)):
        for at in list(blocks):
            sent = blocks[at] if at == 0 or hold is None else after(blocks[at], *hold)
            blocks[at | bit] = swap(sent, bit, count)
    return blocks


def scatter_sums(blocks, count):
    blocks = dict(blocks)
    bits = bits_of(count)
    for bit in bits[:-1]:
        kept = {}
        for at in blocks:
            if not at & bit:
                arrived = swap(blocks[at | bit].astype(jnp.bfloat16), bit, count)
                kept[at] = blocks[at].astype(jnp.float32) + arrived.astype(jnp.float32)
        blocks = kept
    return blocks[0], blocks[bits[-1]].astype(jnp.bfloat16)


def last_swap(sent, count):
    return swap(sent, bits_of(count)[-1], count).astype(jnp.float32)


def scatter_blocks(blocks, count):
    kept, sent = scatter_sums(blocks, count)
    return kept + last_swap(sent, count)


def gather_rows(block, count):
    own = lax.axis_index("fsdp")
    held = [(0, block)]
    stacked = block[None]
    for bit in reversed(bits_of(count)):
        arrived = swap(stacked, bit, count, "fsdp")
        held = held + [(at | bit, arrived[i]) for i, (at, _) in enumerate(held)]
        stacked = jnp.concatenate([stacked, arrived], axis=0)
    rows, width = block.shape
    whole = jnp.zeros((count * rows, width), block.dtype)
    for at, piece in held:
        whole = lax.dynamic_update_slice(whole, piece, ((own ^ at) * rows, 0))
    return whole


def scatter_rows(sums, count):
    own = lax.axis_index("fsdp")
    _, rows, width = sums.shape
    for bit in bits_of(count):
        mine = (own & bit) // bit
        split = sums.reshape(-1, 2, rows, width)
        pick = lambda at: lax.dynamic_index_in_dim(split, at, axis=1, keepdims=False)
        arrived = swap(pick(1 - mine).astype(jnp.bfloat16), bit, count, "fsdp")
        sums = pick(mine).astype(jnp.float32) + arrived.astype(jnp.float32)
    return sums.reshape(rows, width).astype(jnp.bfloat16)


def in_order(blocks, own, count):
    batch, rows, width = blocks[0].shape
    whole = jnp.zeros((batch, count * rows, width), blocks[0].dtype)
    for at in range(count):
        whole = lax.dynamic_update_slice(whole, blocks[at], (0, (own ^ at) * rows, 0))
    return whole


def from_order(whole, own, count):
    rows = whole.shape[1] // count
    return {
        at: lax.dynamic_slice_in_dim(whole, (own ^ at) * rows, rows, axis=1) for at in range(count)
    }


def dot(left, right):
    return jnp.dot(left, right, preferred_element_type=jnp.float32)


def dot_t(left, right):
    return lax.dot_general(
        left, right, (((1,), (1,)), ((), ())), preferred_element_type=jnp.float32
    )


def t_dot(left, right):
    return lax.dot_general(
        left, right, (((0,), (0,)), ((), ())), preferred_element_type=jnp.float32
    )


def per_device(
    fsdp,
    seq,
    tokens,
    w_query,
    w_key,
    w_value,
    w_out,
    w_gate,
    w_up,
    w_down,
    attn_gain,
    ffn_gain,
    qk_gain,
    cotangent,
):
    bf16 = jnp.bfloat16
    f32 = jnp.float32
    own = lax.axis_index("seq")
    batch, rows, width = tokens.shape
    length = rows * seq
    count = batch * length
    part = w_query.shape[0]
    q_width = w_query.shape[1] // seq
    kv_width = w_key.shape[1] // seq
    o_width = w_out.shape[1] // seq
    units = w_down.shape[0] // seq
    local = units * fsdp

    def columns(weight, size):
        return lax.dynamic_slice_in_dim(weight, own * size, size, axis=1)

    gains = jnp.stack([attn_gain, ffn_gain], axis=1)
    first = jnp.concatenate(
        [
            columns(w_query, q_width),
            columns(w_key, kv_width),
            columns(w_value, kv_width),
            columns(w_out, o_width),
            jnp.pad(gains, ((0, 0), (0, 126))),
        ],
        axis=1,
    )
    first_all = gather_rows(first, fsdp)
    qkv_width = q_width + 2 * kv_width
    w_qkv = first_all[:, :qkv_width]
    out_cols = first_all[:, qkv_width : qkv_width + o_width]
    attn_full = first_all[:, qkv_width + o_width].astype(f32)
    ffn_full = first_all[:, qkv_width + o_width + 1].astype(f32)

    def pick(weight):
        split = weight.reshape(part, fsdp, seq, units)
        return lax.dynamic_index_in_dim(split, own, axis=2, keepdims=False).reshape(part, local)

    down_own = lax.dynamic_slice_in_dim(w_down, own * units, units, axis=0)
    second = jnp.concatenate(
        [pick(w_gate), pick(w_up), fold_rows(down_own, part)], axis=1
    )
    second_all = lax.all_gather(second, "fsdp", axis=0, tiled=True)
    down_w = unfold_rows(second_all[:, 2 * local :].reshape(fsdp, part, local), units)
    down_w = down_w.reshape(local, width)

    token_blocks = gather_blocks(tokens, seq)
    inputs_all = in_order(token_blocks, own, seq)
    out_w = lax.all_to_all(out_cols, "seq", split_axis=0, concat_axis=1, tiled=True)

    inputs_all32 = inputs_all.astype(f32)
    scale_all = rms_scale(inputs_all32)
    hat_all = inputs_all32 * scale_all
    normed = (hat_all * attn_full).astype(bf16)
    flat_normed = normed.reshape(count, width)
    qkv_raw = dot(flat_normed, w_qkv).reshape(batch, length, qkv_width)
    tables = head_tables(length, qk_gain)
    query_low, key_low, mixed = attend(qkv_raw, tables)
    flat_mixed = mixed.reshape(count, q_width)
    branch = dot(flat_mixed, out_w).astype(bf16).reshape(batch, length, width)
    cot_blocks = gather_blocks(after(cotangent, *token_blocks.values()), seq, (mixed,))
    cot_all = jnp.concatenate(
        [cot_blocks[at].reshape(batch * rows, width) for at in range(seq)], axis=0
    )
    branch, cot_all = lax.optimization_barrier((branch, cot_all))
    inputs = tokens.astype(f32)
    middle = inputs + scatter_blocks(from_order(branch, own, seq), seq)

    scale_two = rms_scale(middle)
    normed_two = (middle * scale_two * ffn_full).astype(bf16)
    flat = lambda values: values.reshape(batch * rows, width)
    half = seq // 2
    high = bits_of(seq)[-1]
    opposite = swap(normed_two, high, seq)
    near_blocks = gather_blocks(normed_two, half)
    near = jnp.concatenate([flat(near_blocks[at]) for at in range(half)], axis=0)
    *kept, result_near, back_near = ffn(near, cot_all, second_all, down_w, 0, None)
    far_blocks = gather_blocks(after(opposite, back_near), half)
    far = jnp.concatenate([flat(far_blocks[at]) for at in range(half)], axis=0)
    hidden, grad_gate_act, grad_upward, result_far, back_far = ffn(
        far, cot_all, second_all, down_w, half * batch * rows, kept
    )
    two_all = jnp.concatenate([near, far], axis=0)

    def xor_blocks(one, two):
        pieces = [values.reshape(half, batch, rows, width) for values in (one, two)]
        return {at: pieces[at // half][at % half] for at in range(seq)}

    two_kept, two_sent = scatter_sums(xor_blocks(back_near, back_far), seq)
    two_arrived = last_swap(two_sent, seq)
    hidden, grad_gate_act, grad_upward, two_sent = lax.optimization_barrier(
        (hidden, grad_gate_act, grad_upward, two_sent)
    )
    grad_down = t_dot(hidden, cot_all).astype(bf16)
    grad_gate = t_dot(two_all, grad_gate_act).astype(bf16)
    grad_up = t_dot(two_all, grad_upward).astype(bf16)
    grad_down = jax.vmap(lambda piece: fold_rows(piece, part))(grad_down.reshape(fsdp, units, width))
    grad_down = grad_down.reshape(width, local)
    ffn_sums = jnp.concatenate(
        [grad_gate, grad_up, grad_down], axis=1
    )
    two_arrived, ffn_sums = lax.optimization_barrier((two_arrived, ffn_sums))
    grad_two = two_kept + two_arrived
    grad_middle_norm, grad_ffn_gain = norm_back(grad_two, middle, scale_two, ffn_full)
    grad_middle = cotangent.astype(f32) + grad_middle_norm
    grad_branch = grad_middle.astype(bf16)
    branch_blocks = gather_blocks(grad_branch, seq)
    ffn_share = lax.psum_scatter(ffn_sums, "fsdp", scatter_dimension=0, tiled=True)
    result_parts, _ = lax.optimization_barrier(
        ((result_near, result_far), tuple(branch_blocks.values()))
    )
    result = (middle + scatter_blocks(xor_blocks(*result_parts), seq)).astype(bf16)

    branch_all = in_order(branch_blocks, own, seq).reshape(count, width)
    grad_out = t_dot(flat_mixed, branch_all).astype(bf16)
    grad_out_cols = lax.all_to_all(grad_out, "seq", split_axis=1, concat_axis=0, tiled=True)
    grad_mixed = dot_t(branch_all, out_w).astype(bf16).reshape(batch, length, q_width)
    grad_qkv, gain_sums = attend_back(query_low, key_low, qkv_raw, grad_mixed, tables)
    grad_qkv, result = lax.optimization_barrier((grad_qkv, result))
    grad_qkv = grad_qkv.reshape(count, qkv_width)
    normed_back = dot_t(grad_qkv, w_qkv)
    normed_back_low = normed_back.astype(bf16).reshape(batch, length, width)
    grad_attn_gain = jnp.sum(normed_back * hat_all.reshape(count, width), axis=0)
    normed_kept, normed_sent = scatter_sums(from_order(normed_back_low, own, seq), seq)
    normed_arrived = last_swap(normed_sent, seq)

    last = jnp.concatenate([t_dot(flat_normed, grad_qkv).astype(bf16), grad_out_cols], axis=1)
    last_width = last.shape[1]
    gain_sums = gain_sums[:2, :HD] + gain_sums[:2, HD:]
    gain_row = jnp.concatenate(
        [
            jnp.broadcast_to(gain_sums.reshape(1, 2 * HD), (fsdp, 2 * HD)),
            grad_attn_gain.reshape(fsdp, part),
            grad_ffn_gain.reshape(fsdp, part),
        ],
        axis=1,
    ).astype(bf16)
    gain_row = jnp.pad(gain_row[:, None, :], ((0, 0), (0, 15), (0, last_width - gain_row.shape[1])))
    last = jnp.concatenate([last.reshape(fsdp, part, last_width), gain_row], axis=1)
    last_share = scatter_rows(last, fsdp)
    normed_arrived, last_share = lax.optimization_barrier((normed_arrived, last_share))
    grad_normed = normed_kept + normed_arrived
    inputs_norm, _ = norm_back(grad_normed, inputs, rms_scale(inputs), attn_full)
    grad_tokens = grad_middle + inputs_norm
    last_shares = lax.all_gather(last_share, "seq", axis=0, tiled=False).astype(f32)
    share_blocks = gather_blocks(after(ffn_share, last_shares), seq)
    ffn_shares = jnp.zeros((seq,) + ffn_share.shape, bf16)
    for at in range(seq):
        ffn_shares = lax.dynamic_update_slice(
            ffn_shares, share_blocks[at][None], (own ^ at, 0, 0)
        )

    def unpick(piece):
        split = piece.reshape(seq, part, fsdp, units)
        return jnp.transpose(split, (1, 2, 0, 3)).reshape(part, fsdp * seq * units)

    def side_by_side(piece):
        return jnp.transpose(piece, (1, 0, 2)).reshape(part, -1)

    shard_gate = unpick(ffn_shares[:, :, :local]).astype(f32)
    shard_up = unpick(ffn_shares[:, :, local : 2 * local]).astype(f32)
    shard_down = unfold_rows(ffn_shares[:, :, 2 * local :], units).reshape(seq * units, width)
    shard_down = shard_down.astype(f32)
    top = last_shares[:, :part]
    shard_query = side_by_side(top[:, :, :q_width])
    shard_key = side_by_side(top[:, :, q_width : q_width + kv_width])
    shard_value = side_by_side(top[:, :, q_width + kv_width : qkv_width])
    shard_out = side_by_side(top[:, :, qkv_width:])
    gains = jnp.sum(last_shares[:, part], axis=0)
    gain_total = gains[: 2 * HD].reshape(2, HD)
    return (
        result,
        grad_tokens,
        shard_query,
        shard_key,
        shard_value,
        shard_out,
        shard_gate,
        shard_up,
        shard_down,
        gains[2 * HD : 2 * HD + part],
        gains[2 * HD + part : 2 * HD + 2 * part],
        gain_total,
    )


def solution(mesh):
    placed = (
        P("fsdp", "seq", None),
        P("fsdp", None),
        P("fsdp", None),
        P("fsdp", None),
        P("fsdp", None),
        P("fsdp", None),
        P("fsdp", None),
        P("fsdp", None),
        P("fsdp"),
        P("fsdp"),
        P(),
        P("fsdp", "seq", None),
    )
    return jax.shard_map(
        functools.partial(per_device, mesh.shape["fsdp"], mesh.shape["seq"]),
        mesh=mesh,
        in_specs=placed,
        out_specs=(
            P("fsdp", "seq", None),
            P("fsdp", "seq", None),
            P("fsdp", None),
            P("fsdp", None),
            P("fsdp", None),
            P("fsdp", None),
            P("fsdp", None),
            P("fsdp", None),
            P("fsdp", None),
            P("fsdp"),
            P("fsdp"),
            P(),
        ),
        check_vma=False,
    )
```

```python
import functools

import jax
import jax.numpy as jnp
from jax import lax
from jax.experimental import pallas as pl
from jax.experimental.pallas import tpu as pltpu
from jax.sharding import PartitionSpec as P


HD = 64


RMS_EPSILON = 1e-05
ROPE_THETA = 1000000.0


def rms_scale(values):
    return lax.rsqrt(jnp.mean(values * values, axis=-1, keepdims=True) + RMS_EPSILON)


def rope_tables(positions, head_size):
    half_size = head_size // 2
    freqs = ROPE_THETA ** (-(jnp.arange(half_size, dtype=jnp.float32) * 2.0) / head_size)
    angles = positions.astype(jnp.float32)[:, None] * freqs[None, :]
    angles = jnp.concatenate([angles, angles], axis=-1)
    return (jnp.cos(angles), jnp.sin(angles))


def norm_back(grad, values, scale, gain):
    weighted = grad * gain
    grad_values = scale * weighted - values * scale**3 * jnp.mean(
        weighted * values, axis=-1, keepdims=True
    )
    grad_gain = jnp.sum(grad * values * scale, axis=(0, 1))
    return (grad_values, grad_gain)


LANES = 128
BLOCK_ROWS = 256


def low_half(shape):
    return lax.broadcasted_iota(jnp.int32, shape, len(shape) - 1) % LANES < HD


def first_part(shape):
    return lax.broadcasted_iota(jnp.int32, shape, len(shape) - 1) % HD < HD // 2


def pair_scale(raw):
    squares = raw * raw
    low = low_half(raw.shape)
    one = jnp.sum(jnp.where(low, squares, 0.0), axis=1, keepdims=True)
    two = jnp.sum(jnp.where(low, 0.0, squares), axis=1, keepdims=True)
    one = lax.rsqrt(one * (1.0 / HD) + RMS_EPSILON)
    two = lax.rsqrt(two * (1.0 / HD) + RMS_EPSILON)
    return jnp.where(low, one, two)


def pair_turn(raw, gain, cosine, sine):
    normed = raw * pair_scale(raw) * gain
    half = HD // 2
    turned = jnp.where(
        first_part(raw.shape),
        -pltpu.roll(normed, LANES - half, 1),
        pltpu.roll(normed, half, 1),
    )
    return normed * cosine + turned * sine


def pair_turn_back(grad, raw, gain, cosine, sine):
    half = HD // 2
    crossed = grad * sine
    turned = jnp.where(
        first_part(raw.shape),
        pltpu.roll(crossed, LANES - half, 1),
        -pltpu.roll(crossed, half, 1),
    )
    grad_normed = grad * cosine + turned
    scale = pair_scale(raw)
    grad_gain = jnp.sum(grad_normed * raw * scale, axis=0, keepdims=True)
    weighted = grad_normed * gain
    product = weighted * raw
    low = low_half(raw.shape)
    one = jnp.sum(jnp.where(low, product, 0.0), axis=1, keepdims=True) * (1.0 / HD)
    two = jnp.sum(jnp.where(low, 0.0, product), axis=1, keepdims=True) * (1.0 / HD)
    mean = jnp.where(low, one, two)
    return scale * weighted - raw * (scale * scale * scale) * mean, grad_gain


def both_halves(values, group):
    mine = low_half(values.shape) == (group == 0)
    return jnp.where(mine, values, pltpu.roll(values, HD, 1))


def stack_pair(block):
    low = low_half(block.shape)
    return jnp.concatenate([jnp.where(low, block, 0.0), jnp.where(low, 0.0, block)], axis=0)


def mul(left, right, left_dim, right_dim):
    return lax.dot_general(
        left, right, (((left_dim,), (right_dim,)), ((), ())), preferred_element_type=jnp.float32
    )


def unstack_pair(turned):
    rows = turned.shape[1] // 2
    top = lax.broadcasted_iota(jnp.int32, (LANES, rows), 0) < HD
    return jnp.where(top, turned[:, :rows], turned[:, rows:]).T


def causal_block(rows):
    keys = lax.broadcasted_iota(jnp.int32, (rows, 2 * rows), 0)
    queries = lax.broadcasted_iota(jnp.int32, (rows, 2 * rows), 1) % rows
    return keys <= queries


def attend_kernel(
    q_ref, k_ref, v_ref, cos_ref, sin_ref, gain_ref, q_out, k_out, mixed_out, both_k, both_v
):
    group = pl.program_id(1)
    length = q_ref.shape[1]
    rows = min(BLOCK_ROWS, length)
    cosine = cos_ref[...]
    sine = sin_ref[...]
    queries = pair_turn(q_ref[0], gain_ref[0:1, :], cosine, sine).astype(jnp.bfloat16)
    keys = pair_turn(k_ref[0], gain_ref[1:2, :], cosine, sine).astype(jnp.bfloat16)
    q_out[0] = queries
    k_out[0] = keys
    both_k[...] = both_halves(keys.astype(jnp.float32), group).astype(jnp.bfloat16)
    both_v[...] = both_halves(v_ref[0], group).T.astype(jnp.bfloat16)
    diagonal = causal_block(rows)
    for at in range(length // rows):
        start = at * rows
        block = q_out[0, start : start + rows, :].astype(jnp.float32) * HD ** (-0.5)
        pair = stack_pair(block).astype(jnp.bfloat16)
        last = jnp.exp(mul(both_k[start : start + rows, :], pair, 1, 1))
        last = jnp.where(diagonal, last, 0.0)
        total = jnp.sum(last, axis=0, keepdims=True)
        mixed = mul(both_v[:, start : start + rows], last.astype(jnp.bfloat16), 1, 0)
        if at > 0:
            before = jnp.exp(mul(both_k[:start, :], pair, 1, 1))
            total = total + jnp.sum(before, axis=0, keepdims=True)
            mixed = mixed + mul(both_v[:, :start], before.astype(jnp.bfloat16), 1, 0)
        mixed = mixed / total
        mixed_out[0, start : start + rows, :] = unstack_pair(mixed).astype(jnp.bfloat16)


def attend_back_kernel(
    low_q_ref,
    low_k_ref,
    q_ref,
    k_ref,
    v_ref,
    grad_ref,
    cos_ref,
    sin_ref,
    gain_ref,
    grad_out,
    gain_out,
    both_k,
    both_k_turned,
    both_v,
    sum_k,
    sum_v,
    grad_q,
    kept_k,
    kept_v,
):
    group = pl.program_id(1)
    length = q_ref.shape[1]
    rows = min(BLOCK_ROWS, length)
    q_width = grad_out.shape[2] - 2 * LANES
    groups = q_width // LANES
    keys = both_halves(low_k_ref[0].astype(jnp.float32), group)
    both_k[...] = keys.astype(jnp.bfloat16)
    both_k_turned[...] = keys.T.astype(jnp.bfloat16)
    both_v[...] = both_halves(v_ref[0], group).astype(jnp.bfloat16)
    diagonal = causal_block(rows)
    head_scale = HD ** (-0.5)

    for at in range(length // rows):
        start = at * rows
        here = slice(start, start + rows)
        block = low_q_ref[0, here, :].astype(jnp.float32) * head_scale
        pair = stack_pair(block).astype(jnp.bfloat16)
        grad_pair = stack_pair(grad_ref[0, here, :].astype(jnp.float32)).astype(jnp.bfloat16)
        spans = [(here, True)] + ([(slice(0, start), False)] if at > 0 else [])
        parts = []
        total = 0.0
        for span, masked in spans:
            exps = jnp.exp(mul(both_k[span, :], pair, 1, 1))
            if masked:
                exps = jnp.where(diagonal, exps, 0.0)
            total = total + jnp.sum(exps, axis=0, keepdims=True)
            parts.append(exps)
        inverse = 1.0 / total
        inner = 0.0
        both = []
        for (span, masked), exps in zip(spans, parts):
            probs = exps * inverse
            grad_probs = mul(both_v[span, :], grad_pair, 1, 1)
            inner = inner + jnp.sum(probs * grad_probs, axis=0, keepdims=True)
            both.append((probs, grad_probs))
        turned = 0.0
        for (span, masked), (probs, grad_probs) in zip(spans, both):
            grad_scores = (probs * (grad_probs - inner)).astype(jnp.bfloat16)
            add_v = mul(probs.astype(jnp.bfloat16), grad_pair, 1, 0)
            add_k = mul(grad_scores, pair, 1, 0)
            if masked:
                sum_v[span, :] = add_v
                sum_k[span, :] = add_k
            else:
                sum_v[span, :] = sum_v[span, :] + add_v
                sum_k[span, :] = sum_k[span, :] + add_k
            turned = turned + mul(both_k_turned[:, span], grad_scores, 1, 0)
        grad_q[here, :] = unstack_pair(turned) * head_scale

    def low(values):
        return values.astype(jnp.bfloat16).astype(jnp.float32)

    cosine = cos_ref[...]
    sine = sin_ref[...]
    raw_grad, gain_grad = pair_turn_back(
        low(grad_q[...]), q_ref[0], gain_ref[0:1, :], cosine, sine
    )
    grad_out[0, :, pl.ds(pl.multiple_of(group * LANES, LANES), LANES)] = raw_grad.astype(
        jnp.bfloat16
    )

    @pl.when((group == 0) & (pl.program_id(0) == 0))
    def _():
        gain_out[...] = jnp.zeros_like(gain_out)

    gain_out[0:1, :] = gain_out[0:1, :] + gain_grad
    mine = low_half((length, LANES)) == (group == 0)
    whole_k = sum_k[...] + pltpu.roll(sum_k[...], HD, 1)
    whole_v = sum_v[...] + pltpu.roll(sum_v[...], HD, 1)

    @pl.when(group == 0)
    def _():
        kept_k[...] = whole_k
        kept_v[...] = whole_v

    @pl.when(group == groups - 1)
    def _():
        all_k = low(jnp.where(mine, whole_k, kept_k[...]))
        all_v = jnp.where(mine, whole_v, kept_v[...])
        raw_k, gain_k = pair_turn_back(all_k, k_ref[0], gain_ref[1:2, :], cosine, sine)
        grad_out[0, :, q_width : q_width + LANES] = raw_k.astype(jnp.bfloat16)
        grad_out[0, :, q_width + LANES :] = all_v.astype(jnp.bfloat16)
        gain_out[1:2, :] = gain_out[1:2, :] + gain_k


def head_tables(length, qk_gain):
    cosine, sine = rope_tables(jnp.arange(length, dtype=jnp.int32), HD)
    twice = lambda table: jnp.concatenate([table, table], axis=1)
    return twice(cosine), twice(sine), twice(qk_gain.astype(jnp.float32))


def attend(qkv_raw, tables):
    batch, length, width = qkv_raw.shape
    groups = width // LANES - 2
    assert groups == 2
    column = lambda at: pl.BlockSpec((1, length, LANES), lambda b, g: (b, 0, at))
    own_column = pl.BlockSpec((1, length, LANES), lambda b, g: (b, 0, g))
    table = pl.BlockSpec((length, LANES), lambda b, g: (0, 0))
    pairs = batch * groups * length * length
    return pl.pallas_call(
        attend_kernel,
        grid=(batch, groups),
        in_specs=[
            own_column,
            column(groups),
            column(groups + 1),
            table,
            table,
            pl.BlockSpec((2, LANES), lambda b, g: (0, 0)),
        ],
        out_specs=[own_column, column(0), own_column],
        out_shape=[
            jax.ShapeDtypeStruct((batch, length, groups * LANES), jnp.bfloat16),
            jax.ShapeDtypeStruct((batch, length, LANES), jnp.bfloat16),
            jax.ShapeDtypeStruct((batch, length, groups * LANES), jnp.bfloat16),
        ],
        scratch_shapes=[
            pltpu.VMEM((length, LANES), jnp.bfloat16),
            pltpu.VMEM((LANES, length), jnp.bfloat16),
        ],
        cost_estimate=pl.CostEstimate(
            flops=pairs * 512, transcendentals=pairs, bytes_accessed=8 * qkv_raw.size
        ),
        name="attend",
    )(qkv_raw, qkv_raw, qkv_raw, *tables)


def attend_back(query_low, key_low, qkv_raw, grad_mixed, tables):
    batch, length, width = qkv_raw.shape
    groups = width // LANES - 2
    column = lambda at: pl.BlockSpec((1, length, LANES), lambda b, g: (b, 0, at))
    own_column = pl.BlockSpec((1, length, LANES), lambda b, g: (b, 0, g))
    table = pl.BlockSpec((length, LANES), lambda b, g: (0, 0))
    pairs = batch * groups * length * length
    return pl.pallas_call(
        attend_back_kernel,
        grid=(batch, groups),
        in_specs=[
            own_column,
            column(0),
            own_column,
            column(groups),
            column(groups + 1),
            own_column,
            table,
            table,
            pl.BlockSpec((2, LANES), lambda b, g: (0, 0)),
        ],
        out_specs=[
            pl.BlockSpec((1, length, width), lambda b, g: (b, 0, 0)),
            pl.BlockSpec((8, LANES), lambda b, g: (0, 0)),
        ],
        out_shape=[
            jax.ShapeDtypeStruct((batch, length, width), jnp.bfloat16),
            jax.ShapeDtypeStruct((8, LANES), jnp.float32),
        ],
        scratch_shapes=[
            pltpu.VMEM((length, LANES), jnp.bfloat16),
            pltpu.VMEM((LANES, length), jnp.bfloat16),
            pltpu.VMEM((length, LANES), jnp.bfloat16),
        ]
        + [pltpu.VMEM((length, LANES), jnp.float32)] * 5,
        cost_estimate=pl.CostEstimate(
            flops=pairs * 1280, transcendentals=pairs, bytes_accessed=12 * qkv_raw.size
        ),
        name="attend_back",
    )(query_low, key_low, qkv_raw, qkv_raw, qkv_raw, grad_mixed, *tables)


FFN_ROWS = 256


def ffn_kernel(two_ref, cot_ref, gate_w, up_w, down_w, *refs):
    hidden_out, gate_out, up_out, result_out, back_out = refs[-5:]
    two = two_ref[...]
    gate = mul(two, gate_w[...], 1, 0)
    upward = mul(two, up_w[...], 1, 0)
    grad_hidden = mul(cot_ref[...], down_w[...], 1, 1)
    sigma = 1.0 / (1.0 + jnp.exp(-gate))
    activated = gate * sigma
    hidden = (activated * upward).astype(jnp.bfloat16)
    grad_gate = grad_hidden * upward * sigma * (1.0 + gate * (1.0 - sigma))
    grad_gate = grad_gate.astype(jnp.bfloat16)
    grad_up = (grad_hidden * activated).astype(jnp.bfloat16)
    hidden_out[...] = hidden
    gate_out[...] = grad_gate
    up_out[...] = grad_up
    result_out[...] = mul(hidden, down_w[...], 1, 0).astype(jnp.bfloat16)
    back = mul(grad_gate, gate_w[...], 1, 1) + mul(grad_up, up_w[...], 1, 1)
    back_out[...] = back.astype(jnp.bfloat16)


def ffn(two, cot_all, second_all, down_w, first_row, kept):
    rows, width = two.shape
    local = down_w.shape[0]
    step = min(FFN_ROWS, rows)
    offset = first_row // step
    here = lambda size: pl.BlockSpec((step, size), lambda i: (i, 0))
    there = lambda size: pl.BlockSpec((step, size), lambda i: (i + offset, 0))
    whole = lambda shape, at: pl.BlockSpec(shape, lambda i: (0, at))
    total = cot_all.shape[0]
    kept = () if kept is None else kept
    return pl.pallas_call(
        ffn_kernel,
        grid=(rows // step,),
        in_specs=[
            here(width),
            there(width),
            whole((width, local), 0),
            whole((width, local), 1),
            whole((local, width), 0),
        ]
        + [pl.BlockSpec(memory_space=pl.ANY)] * len(kept),
        out_specs=[there(local)] * 3 + [here(width)] * 2,
        out_shape=[jax.ShapeDtypeStruct((total, local), jnp.bfloat16)] * 3
        + [jax.ShapeDtypeStruct((rows, width), jnp.bfloat16)] * 2,
        input_output_aliases={5 + at: at for at in range(len(kept))},
        cost_estimate=pl.CostEstimate(
            flops=12 * rows * width * local,
            transcendentals=rows * local,
            bytes_accessed=2 * (3 * width * local + rows * (4 * width + 3 * local)),
        ),
        name="ffn",
    )(two, cot_all, second_all, second_all, down_w, *kept)


def fold_rows(piece, part):
    units, width = piece.shape
    extra = piece[part:].reshape(units - part, width // LANES, LANES)
    extra = jnp.transpose(extra, (1, 0, 2)).reshape(part, LANES)
    return jnp.concatenate([piece[:part], extra], axis=1)


def unfold_rows(folded, units):
    lead = folded.shape[:-2]
    part = folded.shape[-2]
    width = folded.shape[-1] - LANES
    extra = folded[..., width:].reshape(lead + (width // LANES, units - part, LANES))
    extra = jnp.swapaxes(extra, -3, -2).reshape(lead + (units - part, width))
    return jnp.concatenate([folded[..., :width], extra], axis=-2)


def bits_of(count):
    return [1 << i for i in range(count.bit_length() - 1)]


def swap(values, bit, axis="seq"):
    total = lax.axis_size(axis)
    return lax.ppermute(values, axis, [(i, i ^ bit) for i in range(total)])


def after(value, *others):
    return lax.optimization_barrier((value, others))[0]


def gather_blocks(block, count, hold=None):
    blocks = {0: block}
    for bit in reversed(bits_of(count)):
        for at in list(blocks):
            sent = blocks[at] if at == 0 or hold is None else after(blocks[at], *hold)
            blocks[at | bit] = swap(sent, bit)
    return blocks


def scatter_sums(blocks, count):
    blocks = dict(blocks)
    bits = bits_of(count)
    for bit in bits[:-1]:
        kept = {}
        for at in blocks:
            if not at & bit:
                arrived = swap(blocks[at | bit].astype(jnp.bfloat16), bit)
                kept[at] = blocks[at].astype(jnp.float32) + arrived.astype(jnp.float32)
        blocks = kept
    return blocks[0], blocks[bits[-1]].astype(jnp.bfloat16)


def last_swap(sent, count):
    return swap(sent, bits_of(count)[-1])


def scatter_blocks(blocks, count):
    kept, sent = scatter_sums(blocks, count)
    return kept + last_swap(sent, count).astype(jnp.float32)


def exchange(pieces, own, count, axis, whole):
    rows, width = pieces.shape[1:]
    for at in range(count):
        piece = lax.dynamic_index_in_dim(pieces, own ^ at, axis=0, keepdims=False)
        if at:
            piece = swap(piece, at)
        start = (own ^ at) * (rows, width)[axis]
        whole = lax.dynamic_update_slice(whole, piece, (start, 0) if axis == 0 else (0, start))
    return whole


def scatter_rows(sums, count, waiting):
    own = lax.axis_index("fsdp")
    _, rows, width = sums.shape
    for bit in bits_of(count):
        mine = (own & bit) // bit
        split = sums.reshape(-1, 2, rows, width)
        pick = lambda at: lax.dynamic_index_in_dim(split, at, axis=1, keepdims=False)
        arrived = swap(pick(1 - mine).astype(jnp.bfloat16), bit, "fsdp")
        if bit == 1:
            arrived, waiting = lax.optimization_barrier((arrived, waiting))
        sums = pick(mine).astype(jnp.float32) + arrived.astype(jnp.float32)
    return sums.reshape(rows, width).astype(jnp.bfloat16), waiting


def in_order(blocks, own, count):
    batch, rows, width = blocks[0].shape
    whole = jnp.zeros((batch, count * rows, width), blocks[0].dtype)
    for at in range(count):
        whole = lax.dynamic_update_slice(whole, blocks[at], (0, (own ^ at) * rows, 0))
    return whole


def from_order(whole, own, count):
    rows = whole.shape[1] // count
    return {
        at: lax.dynamic_slice_in_dim(whole, (own ^ at) * rows, rows, axis=1) for at in range(count)
    }


def dot(left, right):
    return jnp.dot(left, right, preferred_element_type=jnp.float32)


def dot_t(left, right):
    return lax.dot_general(
        left, right, (((1,), (1,)), ((), ())), preferred_element_type=jnp.float32
    )


def t_dot(left, right):
    return lax.dot_general(
        left, right, (((0,), (0,)), ((), ())), preferred_element_type=jnp.float32
    )


def step(
    fsdp,
    seq,
    tokens,
    w_query,
    w_key,
    w_value,
    w_out,
    w_gate,
    w_up,
    w_down,
    attn_gain,
    ffn_gain,
    qk_gain,
    cotangent,
):
    bf16 = jnp.bfloat16
    f32 = jnp.float32
    own = lax.axis_index("seq")
    batch, rows, width = tokens.shape
    length = rows * seq
    count = batch * length
    part = w_query.shape[0]
    q_width = w_query.shape[1] // seq
    kv_width = w_key.shape[1] // seq
    o_width = w_out.shape[1] // seq
    units = w_down.shape[0] // seq
    local = units * fsdp

    def columns(weight, size):
        return lax.dynamic_slice_in_dim(weight, own * size, size, axis=1)

    gains = jnp.stack([attn_gain, ffn_gain], axis=1)
    first = jnp.concatenate(
        [
            columns(w_query, q_width),
            columns(w_key, kv_width),
            columns(w_value, kv_width),
            columns(w_out, o_width),
            jnp.pad(gains, ((0, 0), (0, 126))),
        ],
        axis=1,
    )
    first_all = lax.all_gather(first, "fsdp", axis=0, tiled=True)
    qkv_width = q_width + 2 * kv_width
    w_qkv = first_all[:, :qkv_width]
    out_cols = first_all[:, qkv_width : qkv_width + o_width]
    attn_full = first_all[:, qkv_width + o_width].astype(f32)
    ffn_full = first_all[:, qkv_width + o_width + 1].astype(f32)

    def pick(weight):
        split = weight.reshape(part, fsdp, seq, units)
        return lax.dynamic_index_in_dim(split, own, axis=2, keepdims=False).reshape(part, local)

    down_own = lax.dynamic_slice_in_dim(w_down, own * units, units, axis=0)
    second = jnp.concatenate(
        [pick(w_gate), pick(w_up), fold_rows(down_own, part)], axis=1
    )
    second_all = lax.all_gather(after(second, first_all), "fsdp", axis=0, tiled=True)
    down_w = unfold_rows(second_all[:, 2 * local :].reshape(fsdp, part, local), units)
    down_w = down_w.reshape(local, width)

    high = bits_of(seq)[-1]
    far_tokens = swap(tokens, high)
    token_blocks = gather_blocks(tokens, seq // 2)
    far_blocks = gather_blocks(far_tokens, seq // 2)
    token_blocks |= {at | high: far_blocks[at] for at in far_blocks}
    inputs_all = in_order(token_blocks, own, seq)
    out_pieces = out_cols.reshape(seq, q_width, o_width)
    out_w = exchange(out_pieces, own, seq, 1, jnp.zeros((q_width, width), bf16))

    inputs_all32 = inputs_all.astype(f32)
    scale_all = rms_scale(inputs_all32)
    hat_all = inputs_all32 * scale_all
    normed = (hat_all * attn_full).astype(bf16)
    flat_normed = normed.reshape(count, width)
    qkv_raw = dot(flat_normed, w_qkv).reshape(batch, length, qkv_width)
    tables = head_tables(length, qk_gain)
    query_low, key_low, mixed = attend(qkv_raw, tables)
    mixed, out_w = lax.optimization_barrier((mixed, out_w))
    flat_mixed = mixed.reshape(count, q_width)
    branch = dot(flat_mixed, out_w).astype(bf16).reshape(batch, length, width)
    cot_blocks = gather_blocks(after(cotangent, *token_blocks.values()), seq, (mixed,))
    cot_all = jnp.concatenate(
        [cot_blocks[at].reshape(batch * rows, width) for at in range(seq)], axis=0
    )
    branch, cot_all = lax.optimization_barrier((branch, cot_all))
    inputs = tokens.astype(f32)
    middle = inputs + scatter_blocks(from_order(branch, own, seq), seq)

    scale_two = rms_scale(middle)
    normed_two = (middle * scale_two * ffn_full).astype(bf16)
    flat = lambda values: values.reshape(batch * rows, width)
    half = seq // 2
    opposite = swap(normed_two, high)
    near_blocks = gather_blocks(normed_two, half)
    near = jnp.concatenate([flat(near_blocks[at]) for at in range(half)], axis=0)
    *kept, result_near, back_near = ffn(near, cot_all, second_all, down_w, 0, None)
    far_blocks = gather_blocks(after(opposite, back_near), half)
    far = jnp.concatenate([flat(far_blocks[at]) for at in range(half)], axis=0)
    hidden, grad_gate_act, grad_upward, result_far, back_far = ffn(
        far, cot_all, second_all, down_w, half * batch * rows, kept
    )
    two_all = jnp.concatenate([near, far], axis=0)

    def xor_blocks(one, two):
        pieces = [values.reshape(half, batch, rows, width) for values in (one, two)]
        return {at: pieces[at // half][at % half] for at in range(seq)}

    two_kept, two_sent = scatter_sums(xor_blocks(back_near, back_far), seq)
    two_arrived = last_swap(two_sent, seq)
    hidden, grad_gate_act, grad_upward, two_sent = lax.optimization_barrier(
        (hidden, grad_gate_act, grad_upward, two_sent)
    )
    grad_down = t_dot(hidden, cot_all).astype(bf16)
    grad_gate = t_dot(two_all, grad_gate_act).astype(bf16)
    grad_up = t_dot(two_all, grad_upward).astype(bf16)
    grad_down = jax.vmap(lambda piece: fold_rows(piece, part))(grad_down.reshape(fsdp, units, width))
    grad_down = grad_down.reshape(width, local)
    ffn_sums = jnp.concatenate(
        [grad_gate, grad_up, grad_down], axis=1
    )
    two_arrived, ffn_sums = lax.optimization_barrier((two_arrived, ffn_sums))
    grad_two = two_kept + two_arrived.astype(f32)
    grad_middle_norm, grad_ffn_gain = norm_back(grad_two, middle, scale_two, ffn_full)
    grad_middle = cotangent.astype(f32) + grad_middle_norm
    grad_branch = grad_middle.astype(bf16)
    hat_low = after(inputs_all, grad_branch).astype(f32) * scale_all
    hat_low = hat_low.astype(bf16)
    result_kept, result_sent = scatter_sums(
        xor_blocks(*after((result_near, result_far), two_sent)), seq
    )
    result_kept = middle + result_kept
    branch_blocks = gather_blocks(grad_branch, seq, (hat_low, result_kept, result_sent))
    ffn_share = lax.psum_scatter(ffn_sums, "fsdp", scatter_dimension=0, tiled=True)
    result_sent = after(result_sent, *branch_blocks.values())
    result = (result_kept + last_swap(result_sent, seq).astype(f32)).astype(bf16)

    branch_all = in_order(branch_blocks, own, seq).reshape(count, width)
    grad_out = t_dot(flat_mixed, branch_all).astype(bf16)
    out_pieces = jnp.swapaxes(grad_out.reshape(q_width, seq, o_width), 0, 1)
    grad_out_cols = exchange(out_pieces, own, seq, 0, jnp.zeros((width, o_width), bf16))
    grad_mixed = dot_t(branch_all, out_w).astype(bf16).reshape(batch, length, q_width)
    grad_qkv, gain_sums = attend_back(query_low, key_low, qkv_raw, grad_mixed, tables)
    grad_qkv, result = lax.optimization_barrier((grad_qkv, result))
    grad_qkv = grad_qkv.reshape(count, qkv_width)
    normed_back = dot_t(grad_qkv, w_qkv)
    normed_back_low = normed_back.astype(bf16).reshape(batch, length, width)
    grad_attn_gain = jnp.sum(normed_back * hat_low.reshape(count, width).astype(f32), axis=0)
    normed_kept, normed_sent = scatter_sums(from_order(normed_back_low, own, seq), seq)
    normed_arrived = last_swap(normed_sent, seq)

    last = jnp.concatenate([t_dot(flat_normed, grad_qkv).astype(bf16), grad_out_cols], axis=1)
    last_width = last.shape[1]
    gain_sums = gain_sums[:2, :HD] + gain_sums[:2, HD:]
    gain_row = jnp.concatenate(
        [
            jnp.broadcast_to(gain_sums.reshape(1, 2 * HD), (fsdp, 2 * HD)),
            grad_attn_gain.reshape(fsdp, part),
            grad_ffn_gain.reshape(fsdp, part),
        ],
        axis=1,
    ).astype(bf16)
    gain_row = jnp.pad(gain_row[:, None, :], ((0, 0), (0, 15), (0, last_width - gain_row.shape[1])))
    last = jnp.concatenate([last.reshape(fsdp, part, last_width), gain_row], axis=1)
    last_share, ffn_share = scatter_rows(last, fsdp, ffn_share)
    last_shares = lax.all_gather(last_share, "seq", axis=0, tiled=False)
    share_blocks = gather_blocks(ffn_share, seq)
    grad_normed = normed_kept + after(normed_arrived, last_shares).astype(f32)
    inputs_norm, _ = norm_back(grad_normed, inputs, rms_scale(inputs), attn_full)
    grad_tokens = grad_middle + inputs_norm
    ffn_shares = jnp.zeros((seq,) + ffn_share.shape, bf16)
    for at in range(seq):
        ffn_shares = lax.dynamic_update_slice(
            ffn_shares, share_blocks[at][None], (own ^ at, 0, 0)
        )

    def unpick(piece):
        split = piece.reshape(seq, part, fsdp, units)
        return jnp.transpose(split, (1, 2, 0, 3)).reshape(part, fsdp * seq * units)

    def side_by_side(piece):
        return jnp.concatenate([piece[at] for at in range(seq)], axis=1).astype(f32)

    shard_gate, shard_up = lax.optimization_barrier(
        (unpick(ffn_shares[:, :, :local]), unpick(ffn_shares[:, :, local : 2 * local]))
    )
    shard_gate, shard_up = shard_gate.astype(f32), shard_up.astype(f32)
    shard_down = unfold_rows(ffn_shares[:, :, 2 * local :], units).reshape(seq * units, width)
    shard_down = shard_down.astype(f32)
    top = last_shares[:, :part]
    shard_query = side_by_side(top[:, :, :q_width])
    shard_key = side_by_side(top[:, :, q_width : q_width + kv_width])
    shard_value = side_by_side(top[:, :, q_width + kv_width : qkv_width])
    shard_out = side_by_side(top[:, :, qkv_width:])
    gains = jnp.sum(last_shares[:, part].astype(f32), axis=0)
    gain_total = gains[: 2 * HD].reshape(2, HD)
    return (
        result,
        grad_tokens,
        shard_query,
        shard_key,
        shard_value,
        shard_out,
        shard_gate,
        shard_up,
        shard_down,
        gains[2 * HD : 2 * HD + part],
        gains[2 * HD + part : 2 * HD + 2 * part],
        gain_total,
    )


def solution(mesh):
    placed = (
        P("fsdp", "seq", None),
        P("fsdp", None),
        P("fsdp", None),
        P("fsdp", None),
        P("fsdp", None),
        P("fsdp", None),
        P("fsdp", None),
        P("fsdp", None),
        P("fsdp"),
        P("fsdp"),
        P(),
        P("fsdp", "seq", None),
    )
    return jax.shard_map(
        functools.partial(step, mesh.shape["fsdp"], mesh.shape["seq"]),
        mesh=mesh,
        in_specs=placed,
        out_specs=(
            P("fsdp", "seq", None),
            P("fsdp", "seq", None),
            P("fsdp", None),
            P("fsdp", None),
            P("fsdp", None),
            P("fsdp", None),
            P("fsdp", None),
            P("fsdp", None),
            P("fsdp", None),
            P("fsdp"),
            P("fsdp"),
            P(),
        ),
        check_vma=False,
    )
```
